256 devices in a mesh: leaf: 64 (over z, x, core), col: 4 (over y).
Axes of the slice: x: 4, y: 4, z: 8, core: 2. Of those that a mesh axis runs over, the one named last changes fastest.
Arguments:
- leaf_rhs: bfloat16 [64, 2048, 512], P('leaf', 'col'), may hold values from -6 to 6
- leaf_inverse: bfloat16 [64, 2048, 2048], P('leaf', None, 'col'), may hold values from -1 to 2, as said below
- panels: bfloat16 [64, 6, 128, 2048], P('leaf', None, None, 'col'), may hold values from -1 to 1
- pattern: int32 [64, 6], P('leaf'), may hold values 0 or 1
- offsets: int32 [64, 6], P('leaf'), may hold values from 0 to 128
- sep_inverse: float32 [64, 6, 256, 256], P('leaf'), may hold values from -2 to 2, as said below
- sep_link: float32 [64, 5, 256, 256], P('leaf'), may hold values from -1 to 1, as said below
- sep_rhs: float32 [64, 6, 256, 512], P('leaf'), may hold values from -4 to 4, as said below
Outputs:
- leaf_solution: bfloat16 [64, 2048, 512], P('leaf', 'col')
- sep_solution: float32 [64, 6, 256, 512], P('leaf', None, None, 'col')
The draws below stay inside these ranges and needn't reach their ends.
Inputs may be any that keep to these rules, and one draw needn't show every extreme that they name: `pattern`: 1 where a leaf couples to its ancestor separator of that level, else 0. A coupling block touches rows offsets to offsets + 127 of its separator. `leaf_inverse`: each block is lower triangular with diagonal entries between 0.5 and 1.5. `sep_inverse`: each block is lower triangular with diagonal entries between 0.5 and 1.5; entries [i, k] are equal for all leaves i of one level-k node, the 2^(k+1) leaves that share i // 2^(k+1). `sep_link`: entries [i, k] are equal for all leaves i that share i // 2^(k+1). `sep_rhs`: entries [i, k] are equal for all leaves i that share i // 2^(k+1).
All inputs are finite; a program needn't handle non-finite values. No bound on the sum of `pattern` on one device may be relied on, other than what follows from the above.
Results may differ from the reference program's by a relative error of at most 0.0062.
Values may be sent and summed in bfloat16 or wider, within the bound.
A program may use at most 64 MiB of HBM per device.

```python
import jax
import jax.numpy as jnp
from jax import lax

LEAF = 2048
SEP = 256
PR = 128
NRHS = 512
LEVELS = 6
N_LEAF = 64


def group_copies(base):
    leaves = jnp.arange(N_LEAF)
    copies = []
    for height in range(base.shape[1]):
        first_leaf = leaves // 2 ** (height + 1) * 2 ** (height + 1)
        copies.append(jnp.take(base[:, height], first_leaf, axis=0))
    return jnp.stack(copies, axis=1)


def triangular(key, count, order, spread):
    normals = jnp.clip(jax.random.normal(key, (count, order, order), jnp.float32), -4.0, 4.0)
    row_ids = lax.broadcasted_iota(jnp.int32, (order, order), 0)
    col_ids = lax.broadcasted_iota(jnp.int32, (order, order), 1)
    lower_part = (row_ids > col_ids).astype(jnp.float32)
    identity = (row_ids == col_ids).astype(jnp.float32)
    diag_vals = jax.random.uniform(jax.random.fold_in(key, 7), (count, order, 1), jnp.float32, 0.5, 1.5)
    return normals * lower_part * (spread / order ** 0.5) + identity * diag_vals


def draw_leaf_inverse(key, part):
    keys = jax.random.split(key, N_LEAF)
    return lax.map(lambda single: triangular(single, 1, LEAF, 1.0)[0].astype(jnp.bfloat16), keys)


def draw_panels(key, part):
    normals = jnp.clip(jax.random.normal(key, (N_LEAF, LEVELS, PR, LEAF), jnp.float32), -4.0, 4.0)
    scales = 1.5 / jnp.sqrt(LEAF * 2.0 ** (jnp.arange(LEVELS).astype(jnp.float32) + 1.0))
    return (normals * scales[None, :, None, None]).astype(jnp.bfloat16)


def draw_sep_inverse(key, part):
    spread = 1.0
    base = triangular(key, N_LEAF * LEVELS, SEP, spread).reshape(N_LEAF, LEVELS, SEP, SEP)
    return group_copies(base)


def draw_sep_link(key, part):
    normals = jnp.clip(jax.random.normal(key, (N_LEAF, LEVELS - 1, SEP, SEP), jnp.float32), -4.0, 4.0)
    return group_copies(normals * (0.7 / SEP ** 0.5))


def draw_sep_rhs(key, part):
    values = jnp.clip(jax.random.normal(key, (N_LEAF, LEVELS, SEP, NRHS), jnp.float32), -4.0, 4.0)
    return group_copies(values)


def with_ends(drawn, rng, least, top_value):
    longest = drawn.shape.index(max(drawn.shape))
    spots = []
    for shift in (0, 1):
        where = [jax.random.randint(jax.random.fold_in(rng, axis), (), 0, length) for axis, length in enumerate(drawn.shape)]
        where[longest] = (where[longest] + shift) % drawn.shape[longest]
        spots.append(tuple(where))
    return drawn.at[spots[0]].set(least).at[spots[1]].set(top_value)


def steps_of(key, extent, cuts, least, top_value):
    level = 1.0
    for position, parts in cuts:
        steps = jax.random.uniform(jax.random.fold_in(jax.random.fold_in(key, 6), position), (parts,), jnp.float32, least / len(cuts), top_value / len(cuts))
        level = level * jnp.repeat(jnp.exp(steps), extent[position] // parts).reshape((-1,) + (1,) * (len(extent) - 1 - position))
    return level


def centred(own_key, shape, scale, reach, pieces=(), dtype=jnp.bfloat16):
    drawn = jax.random.normal(own_key, shape, jnp.float32) * scale
    if len(pieces) > 0:
        drawn = steps_of(own_key, shape, pieces, -0.22, 0.18) * drawn
    return jnp.clip(drawn, min=-reach, max=reach).astype(dtype)


def setup_inputs(seed: int = 0) -> dict:
    key_list = jax.random.split(jax.random.key(seed), 9)
    return {
        "leaf_rhs": centred(key_list[0], (N_LEAF, LEAF, NRHS), 1.0, 6.0, ((0, 64), (1, 4))),
        "leaf_inverse": draw_leaf_inverse(jax.random.fold_in(key_list[8], 71), 0),
        "panels": draw_panels(jax.random.fold_in(key_list[8], 71), 0),
        "pattern": with_ends((jax.random.randint(key_list[3], (N_LEAF, LEVELS), 0, 4) < 3).astype(jnp.int32), jax.random.fold_in(key_list[3], 1), 0, 1),
        "offsets": with_ends(jax.random.randint(key_list[4], (N_LEAF, LEVELS), 0, SEP - PR + 1), jax.random.fold_in(key_list[4], 1), 0, SEP - PR).astype(jnp.int32),
        "sep_inverse": draw_sep_inverse(jax.random.fold_in(key_list[8], 71), 0),
        "sep_link": draw_sep_link(jax.random.fold_in(key_list[8], 71), 0),
        "sep_rhs": draw_sep_rhs(jax.random.fold_in(key_list[8], 71), 0),
    }


def forward_leaf(members):
    inverse_blk, right_blk, panel_blk = members
    solved_blk = jnp.dot(inverse_blk, right_blk, preferred_element_type=jnp.float32).astype(jnp.bfloat16)
    partial_blk = jnp.einsum("kpr,rn->kpn", panel_blk.astype(jnp.float32), solved_blk.astype(jnp.float32))
    return solved_blk, partial_blk


def place_block(partial_blk, first_row, coupling_on):
    zeros_blk = jnp.zeros((SEP, NRHS), jnp.float32)
    return lax.dynamic_update_slice(zeros_blk, coupling_on * partial_blk, (first_row.astype(jnp.int32), jnp.int32(0)))


def slice_block(sep_blk, first_row):
    return lax.dynamic_slice(sep_blk, (first_row.astype(jnp.int32), jnp.int32(0)), (PR, NRHS))


def backward_leaf(members):
    inverse_blk, solved_blk, panel_blk, rounded_blk, first_rows, pattern_row = members
    sliced = jax.vmap(slice_block)(rounded_blk, first_rows)
    sliced = sliced * pattern_row.astype(jnp.bfloat16)[:, None, None]
    coupled = jnp.einsum("kpr,kpn->rn", panel_blk.astype(jnp.float32), sliced.astype(jnp.float32))
    reduced = (solved_blk.astype(jnp.float32) - coupled).astype(jnp.bfloat16)
    final = lax.dot_general(inverse_blk, reduced, (((0,), (0,)), ((), ())), preferred_element_type=jnp.float32)
    return final.astype(jnp.bfloat16)


def reference(leaf_rhs, leaf_inverse, panels, pattern, offsets, sep_inverse, sep_link, sep_rhs):
    highest = lax.Precision.HIGHEST
    solved, partial_value = lax.map(forward_leaf, (leaf_inverse, leaf_rhs, panels))
    coupling_on = pattern.astype(jnp.float32)
    placed = jax.vmap(jax.vmap(place_block))(partial_value, offsets, coupling_on)
    forward_sols = []
    for height in range(LEVELS):
        group_size = 2 ** (height + 1)
        update = placed[:, height].reshape(N_LEAF // group_size, group_size, SEP, NRHS).sum(axis=1)
        if height > 0:
            half_size = group_size // 2
            linked = jnp.einsum("jab,jbn->jan", sep_link[::half_size, height - 1], forward_sols[height - 1], precision=highest)
            update = update + linked.reshape(N_LEAF // group_size, 2, SEP, NRHS).sum(axis=1)
        right_nodes = sep_rhs[::group_size, height]
        forward_sols.append(jnp.einsum("jab,jbn->jan", sep_inverse[::group_size, height], right_nodes - update, precision=highest))
    backward_sols = [None] * LEVELS
    for height in reversed(range(LEVELS)):
        group_size = 2 ** (height + 1)
        residue = forward_sols[height]
        if height + 1 < LEVELS:
            parent_sol = jnp.repeat(backward_sols[height + 1], 2, axis=0)
            residue = residue - jnp.einsum("jba,jbn->jan", sep_link[::group_size, height], parent_sol, precision=highest)
        backward_sols[height] = jnp.einsum("jba,jbn->jan", sep_inverse[::group_size, height], residue, precision=highest)
    sep_solution = jnp.stack([jnp.repeat(backward_sols[height], 2 ** (height + 1), axis=0) for height in range(LEVELS)], axis=1)
    rounded = sep_solution.astype(jnp.bfloat16)
    leaf_solution = lax.map(backward_leaf, (leaf_inverse, solved, panels, rounded, offsets, pattern))
    return leaf_solution, sep_solution
```

```python
import functools

import jax
import jax.numpy as jnp
from jax import lax
from jax.experimental import pallas as pl
from jax.experimental.pallas import tpu as pltpu
from jax.sharding import PartitionSpec as P

MESH = pl.DeviceIdType.MESH
F32 = jnp.float32
BF16 = jnp.bfloat16
HOP = BF16
LEVELS = 6
MASKS = (1, 2, 6, 8, 16, 56)
PAIRS = tuple((k, j) for k in range(1, LEVELS) for j in range(k, LEVELS))


def dot_nn(a, b):
    return lax.dot_general(a, b, (((1,), (0,)), ((), ())), preferred_element_type=F32)


def dot_nt(a, b):
    return lax.dot_general(a, b, (((1,), (1,)), ((), ())), preferred_element_type=F32)


def halves(value):
    high = value.astype(BF16)
    return high, (value - high.astype(F32)).astype(BF16)


def wide(value):
    high, low = halves(value)
    return jnp.concatenate([high, low, high], axis=1)


def kernel(
    rhs, inv, pan, pat, off, sinv, slink, srhs, x_out, sol_out,
    rhs_v, inv_v, pan_v, sinv_v, slink_v, srhs_v,
    bt, fp, fsnd, frx, sol_v, cc, cb, prl, psum, prx, pon, meta, metarx, est,
    wf, wi, wg, rt, u, fs, bs, tsnd, trx, ball, soth, sall, redv, xacc,
    ld, f_ss, f_rs, p_ss, p_rs, prx_rs, m_ss, m_rs, t_ss, t_rs, b_ss, b_rs, s_ss, s_rs, r_ss, r_rs,
):
    leaf = lax.axis_index("leaf")
    c = lax.axis_index("col")
    q = lax.rem(leaf, 2)
    base = leaf - q
    c1, c2, c3 = lax.rem(c + 1, 4), lax.rem(c + 2, 4), lax.rem(c + 3, 4)
    rows = 512

    def remote(src, dst, ss, rs, to_leaf, to_col):
        return pltpu.make_async_remote_copy(
            src_ref=src, dst_ref=dst, send_sem=ss, recv_sem=rs,
            device_id=(to_leaf, to_col), device_id_type=MESH,
        )

    sent = []

    def on(cond, fn):
        pl.when(cond)(fn)

    def order(step):
        return jnp.where(c == 0, (2, 1, 3, 0)[step], 3 - step)

    load_rhs = pltpu.make_async_copy(rhs, rhs_v, ld.at[0])
    load_rhs.start()
    load_inv = []
    for step in range(4):
        r = jnp.maximum(order(step), 0)
        load_inv.append(
            pltpu.make_async_copy(inv.at[pl.ds(pl.multiple_of(r * rows, rows), rows)], inv_v.at[r], ld.at[1 + step])
        )
        on(step <= 3 - c, load_inv[step].start)
    load_pan = pltpu.make_async_copy(pan, pan_v, ld.at[5])
    load_pan.start()
    load_sinv = pltpu.make_async_copy(sinv, sinv_v, ld.at[6])
    load_sinv.start()
    load_slink = pltpu.make_async_copy(slink, slink_v, ld.at[7])
    load_slink.start()
    load_srhs = pltpu.make_async_copy(
        srhs.at[:, :, pl.ds(pl.multiple_of(c * 128, 128), 128)], srhs_v, ld.at[8]
    )
    load_srhs.start()

    peers = [(leaf, c1), (leaf, c2), (leaf, c3)]
    peers += [(base + 1 - q, cc_) for cc_ in (c, c1, c2, c3)]
    peers += [(leaf ^ MASKS[k], c) for k in range(1, LEVELS)]
    barrier = pltpu.get_barrier_semaphore()
    for peer in peers:
        pl.semaphore_signal(barrier, inc=1, device_id=peer, device_id_type=MESH)

    for k in range(LEVELS):
        meta[pl.ds(k, 1), :] = jnp.full((1, 256), off[0, k].astype(F32), F32)
        meta[pl.ds(8 + k, 1), :] = jnp.full((1, 256), pat[0, k].astype(F32), F32)

    load_rhs.wait()
    bt[...] = rhs_v[...].T
    pl.semaphore_wait(barrier, len(peers))

    other = base + 1 - q
    send_meta = remote(meta, metarx, m_ss, m_rs, other, c)
    send_meta.start()

    def fmsg(sender, number, src, slot, to_col):
        return (c == sender, remote(src, frx.at[slot], f_ss.at[number], f_rs.at[slot], leaf, to_col))

    msgs = {
        "20A": fmsg(0, 0, fsnd.at[0, 0], 0, 1),
        "20B": fmsg(0, 1, fsnd.at[0, 1], 0, 3),
        "10A": fmsg(0, 2, fsnd.at[1, 0], 1, 1),
        "10B": fmsg(0, 3, fsnd.at[1, 1], 2, 1),
        "30A": fmsg(0, 4, fsnd.at[2, 0], 1, 3),
        "30B": fmsg(0, 5, fsnd.at[2, 1], 2, 3),
        "31A": fmsg(1, 0, fsnd.at[0, 0], 0, 0),
        "31B": fmsg(1, 1, fsnd.at[0, 1], 1, 0),
        "21B": fmsg(1, 2, fsnd.at[1, 1], 0, 2),
        "21A": fmsg(1, 3, fsnd.at[1, 0], 1, 2),
        "32A": fmsg(2, 0, fsnd.at[0, 0], 3, 3),
        "32B": fmsg(2, 1, fsnd.at[0, 1], 4, 3),
        "relay": fmsg(3, 0, frx.at[0], 2, 2),
    }
    now = {
        (0, 0): ("20A", "31A", "32A"),
        (0, 1): ("20B", "31B", "32B"),
        (1, 0): ("10A",),
        (1, 1): ("10B", "21B"),
    }
    for step in range(4):

        def block(step=step):
            load_inv[step].wait()
            r = order(step)
            for h in range(2):
                value = dot_nt(bt[pl.ds(h * 256, 256), :], inv_v[r])
                fp[step, h] = value
                if step < 3:
                    fsnd[step, h] = value.astype(BF16)
                for name in now.get((step, h), ()):
                    cond, copy = msgs[name]
                    on(cond, copy.start)

        on(step <= 3 - c, block)

    load_sinv.wait()
    load_slink.wait()
    load_srhs.wait()
    highest = lax.Precision.HIGHEST

    def table(k, carry):
        ik = sinv_v[k]
        kk = jnp.minimum(k, LEVELS - 2)
        gk = lax.dot_general(
            slink_v[kk], ik, (((1,), (0,)), ((), ())), precision=highest, preferred_element_type=F32
        )
        ih, il = halves(ik)
        gh, gl = halves(gk)
        for at, (hi, lo) in ((0, (ih, il)), (256, (gh, gl))):
            wf[k, pl.ds(at, 256), pl.ds(0, 256)] = hi
            wf[k, pl.ds(at, 256), pl.ds(256, 256)] = hi
            wf[k, pl.ds(at, 256), pl.ds(512, 256)] = lo
        for ref, (hi, lo) in ((wi, (ih, il)), (wg, (gh, gl))):
            ref[k, pl.ds(0, 256), :] = hi
            ref[k, pl.ds(256, 256), :] = hi
            ref[k, pl.ds(512, 256), :] = lo
        rt[k] = srhs_v[k].T
        return carry

    lax.fori_loop(0, LEVELS, table, 0)

    send_meta.wait_recv()
    gap = (
        lax.broadcasted_iota(jnp.int32, (128, 256), 1) - lax.broadcasted_iota(jnp.int32, (128, 256), 0)
    ).astype(F32)
    for k in range(LEVELS):
        for part, ref in enumerate((meta, metarx)):
            spot = jnp.broadcast_to(ref[pl.ds(k, 1), :], (128, 256))
            keep = jnp.broadcast_to(ref[pl.ds(8 + k, 1), :], (128, 256))
            hot = jnp.where(gap == spot, keep, 0.0).astype(BF16)
            est[k, pl.ds(part * 256, 128), :] = hot
            est[k, pl.ds(part * 256 + 128, 128), :] = hot

    def frecv(slot, from_col):
        remote(frx.at[slot], frx.at[slot], f_ss.at[0], f_rs.at[slot], leaf, from_col).wait_recv()

    def after0():
        for h, name in enumerate(("30A", "30B")):
            frecv(h, 1)
            fsnd[2, h] = (fp[2, h] + frx[h].astype(F32)).astype(BF16)
            msgs[name][1].start()
        for h in range(2):
            sol_v[0, h] = fp[3, h].astype(BF16)

    def after1():
        frecv(0, 0)
        fsnd[1, 0] = (fp[1, 0] + frx[0].astype(F32)).astype(BF16)
        msgs["21A"][1].start()
        for h in range(2):
            frecv(1 + h, 0)
            sol_v[1, h] = (fp[2, h] + frx[1 + h].astype(F32)).astype(BF16)

    def after2():
        frecv(1, 1)
        sol_v[2, 0] = (fp[1, 0] + frx[1].astype(F32)).astype(BF16)
        frecv(0, 1)
        frecv(2, 3)
        sol_v[2, 1] = (fp[1, 1] + frx[0].astype(F32) + frx[2].astype(F32)).astype(BF16)

    def after3():
        frecv(0, 0)
        msgs["relay"][1].start()
        for h in range(2):
            frecv(3 + h, 2)
            frecv(1 + h, 0)
            sol_v[3, h] = (fp[0, h] + frx[1 + h].astype(F32) + frx[3 + h].astype(F32)).astype(BF16)

    for group, fn in enumerate((after0, after1, after2, after3)):
        on(c == group, fn)

    load_pan.wait()
    panels = pan_v
    for h in range(2):
        share = dot_nt(sol_v[c, h], panels[...]).reshape(2, 2, 64, 768)
        cc[pl.ds(2 * h, 2)] = share
        cb[pl.ds(2 * h, 2)] = share.astype(BF16)
    relay_up = remote(cb.at[c2, 0], prl.at[0], p_ss.at[0], p_rs.at[0], leaf, c1)
    relay_down = remote(cb.at[c2, 1], prl.at[1], p_ss.at[1], p_rs.at[1], leaf, c3)
    direct_up = remote(cb.at[c1, 1], prx.at[q, 0], p_ss.at[2], prx_rs.at[q, 0], base + 1, c1)
    direct_down = remote(cb.at[c3, 0], prx.at[q, 1], p_ss.at[3], prx_rs.at[q, 1], base, c3)
    across = remote(cb.at[c, 1 - q], pon, p_ss.at[4], p_rs.at[2], other, c)
    sum_up = remote(psum.at[0], prx.at[q, 0], p_ss.at[5], prx_rs.at[q, 0], base, c1)
    sum_down = remote(psum.at[1], prx.at[q, 1], p_ss.at[6], prx_rs.at[q, 1], base + 1, c3)
    for copy in (relay_up, relay_down, direct_up, direct_down, across):
        copy.start()
    relay_up.wait_recv()
    psum[0] = (cc[c1, 0] + prl[0].astype(F32)).astype(BF16)
    sum_up.start()
    relay_down.wait_recv()
    psum[1] = (cc[c3, 1] + prl[1].astype(F32)).astype(BF16)
    sum_down.start()
    across.wait_recv()

    def precv(p, d, from_col):
        remote(prx.at[p, d], prx.at[p, d], p_ss.at[0], prx_rs.at[p, d], base + p, from_col).wait_recv()

    for p in range(2):
        precv(p, 0, c3)
        precv(p, 1, c1)
    mine = cc[c, q] + prx[q, 0].astype(F32) + prx[q, 1].astype(F32)
    theirs = pon[...].astype(F32) + prx[1 - q, 0].astype(F32) + prx[1 - q, 1].astype(F32)
    mh, ml = halves(mine)
    th, tl = halves(theirs)
    for k in range(LEVELS):
        at = slice(k * 128, k * 128 + 128)
        left = jnp.concatenate([mh[:, at], ml[:, at], th[:, at], tl[:, at]], axis=1)
        u[k] = dot_nn(left, est[k])

    mine_rows = pl.ds(pl.multiple_of(q * 64, 64), 64)

    def tree(k, j):
        n = PAIRS.index((k, j))
        return remote(tsnd.at[n], trx.at[n], t_ss.at[n], t_rs.at[n], leaf ^ MASKS[k], c)

    def send(k, j):
        tsnd[PAIRS.index((k, j))] = u[j].astype(HOP)
        tree(k, j).start()

    def receive(k, j):
        tree(k, j).wait_recv()
        u[j] = u[j] + trx[PAIRS.index((k, j))].astype(F32)

    for k in range(LEVELS):
        if k > 0:
            receive(k, k)
        both = dot_nt(wide(rt[k, mine_rows, :] - u[k]), wf[k])
        if k + 1 < LEVELS:
            if k > 0:
                receive(k, k + 1)
            u[k + 1] = u[k + 1] + both[:, 256:]
            send(k + 1, k + 1)
            for j in range(k + 2, LEVELS):
                if k > 0:
                    receive(k, j)
                send(k + 1, j)
        fs[k] = dot_nn(wide(both[:, :256]), wi[k])
    for k in reversed(range(LEVELS)):
        down = fs[k]
        if k + 1 < LEVELS:
            down = down - dot_nn(wide(bs[k + 1]), wg[k])
        bs[k] = down
        ball[k, mine_rows, :] = down

    swap = remote(ball.at[:, mine_rows, :], ball.at[:, mine_rows, :], b_ss, b_rs, other, c)
    slot = c * 2 + q
    for k in range(LEVELS):
        low = bs[k].astype(BF16)
        at = slice(k * 128, k * 128 + 128)
        sall[slot, :, at] = dot_nt(low, est[k, pl.ds(0, 128), :]).astype(BF16)
        soth[:, at] = dot_nt(low, est[k, pl.ds(256, 128), :]).astype(BF16)
    s_copies = [
        remote(sall.at[slot], sall.at[slot], s_ss.at[0], s_rs.at[slot], leaf, c1),
        remote(soth, sall.at[slot], s_ss.at[1], s_rs.at[slot], other, c1),
        remote(sall.at[slot], sall.at[slot], s_ss.at[2], s_rs.at[slot], leaf, c3),
        remote(soth, sall.at[slot], s_ss.at[3], s_rs.at[slot], other, c3),
        remote(soth, sall.at[slot], s_ss.at[4], s_rs.at[slot], other, c),
    ]
    for copy in s_copies:
        copy.start()
    swap.start()

    def srecv(at, from_leaf, from_col):
        remote(sall.at[at], sall.at[at], s_ss.at[0], s_rs.at[at], from_leaf, from_col).wait_recv()

    near, far = jnp.where(q == 0, c3, c1), jnp.where(q == 0, c1, c3)
    relays = []
    for p in range(2):
        at = near * 2 + p
        srecv(at, base + p, near)
        relays.append(remote(sall.at[at], sall.at[at], s_ss.at[5 + p], s_rs.at[at], leaf, far))
        relays[p].start()

    remote(ball.at[:, mine_rows, :], ball.at[:, mine_rows, :], b_ss, b_rs, other, c).wait_send()
    theirs_rows = pl.ds(pl.multiple_of((1 - q) * 64, 64), 64)
    remote(ball.at[:, theirs_rows, :], ball.at[:, theirs_rows, :], b_ss, b_rs, other, c).wait_recv()
    for k in range(LEVELS):
        sol_out[k] = ball[k].T

    srecv(c * 2 + 1 - q, other, c)
    for p in range(2):
        srecv(far * 2 + p, base + p, far)
    for p in range(2):
        srecv(c2 * 2 + p, leaf, near)

    for h in range(2):
        taken = sall[pl.ds(4 * h, 4)].reshape(256, 768)
        redv[c, h] = (sol_v[c, h].astype(F32) - dot_nn(taken, panels[...])).astype(BF16)

    def rmsg(sender, number, r, h, to_col):
        return (c == sender, remote(redv.at[r, h], redv.at[r, h], r_ss.at[number], r_rs.at[r, h], leaf, to_col))

    rfirst = [
        rmsg(3, 0, 3, 1, 0), rmsg(3, 1, 3, 0, 0), rmsg(3, 2, 3, 0, 2), rmsg(3, 3, 3, 1, 2),
        rmsg(2, 0, 2, 1, 3), rmsg(2, 1, 2, 0, 1), rmsg(2, 2, 2, 1, 1),
        rmsg(1, 0, 1, 0, 0), rmsg(1, 1, 1, 1, 0),
    ]
    rnext = [rmsg(3, 4, 2, 1, 0), rmsg(2, 3, 3, 0, 1), rmsg(1, 2, 2, 0, 0), rmsg(0, 0, 3, 1, 1)]
    for cond, copy in rfirst:
        on(cond, copy.start)
    for h in range(2):
        xacc[h] = dot_nn(redv[c, h], inv_v[c])

    def rrecv(r, h):
        remote(redv.at[r, h], redv.at[r, h], r_ss.at[0], r_rs.at[r, h], leaf, c1).wait_recv()

    for (cond, copy), (r, h) in zip(rnext, ((2, 1), (3, 0), (2, 0), (3, 1))):

        def pass_on(copy=copy, r=r, h=h):
            rrecv(r, h)
            copy.start()

        on(cond, pass_on)
    for step in range(1, 4):

        def add(step=step):
            r = c + step
            for h in range(2):
                taken = ((c == 2) & (r == 3) & (h == 0)) | ((c == 1) & (r == 2) & (h == 0)) | ((c == 0) & (r == 3) & (h == 1))
                on(jnp.logical_not(taken), functools.partial(rrecv, r, h))
                xacc[h] += dot_nn(redv[r, h], inv_v[r])

        on(c + step <= 3, add)
    for h in range(2):
        x_out[:, pl.ds(h * 256, 256)] = xacc[h].T.astype(BF16)

    for copy in (send_meta, relay_up, relay_down, direct_up, direct_down, across, sum_up, sum_down, *s_copies, *relays):
        copy.wait_send()
    for k, j in PAIRS:
        tree(k, j).wait_send()
    for cond, copy in (*msgs.values(), *rfirst, *rnext):
        on(cond, copy.wait_send)


def on_device(leaf_rhs, leaf_inverse, panels, pattern, offsets, sep_inverse, sep_link, sep_rhs):
    anywhere = pl.BlockSpec(memory_space=pl.ANY)
    scalars = pl.BlockSpec(memory_space=pltpu.SMEM)
    vmem = pl.BlockSpec(memory_space=pltpu.VMEM)
    dma = pltpu.SemaphoreType.DMA
    messages = len(PAIRS)
    x, sol = pl.pallas_call(
        kernel,
        out_shape=(jax.ShapeDtypeStruct((512, 512), BF16), jax.ShapeDtypeStruct((6, 256, 128), F32)),
        in_specs=[anywhere, anywhere, anywhere, scalars, scalars, anywhere, anywhere, anywhere],
        out_specs=(vmem, vmem),
        scratch_shapes=[
            pltpu.VMEM((512, 512), BF16),
            pltpu.VMEM((4, 512, 512), BF16),
            pltpu.VMEM((768, 512), BF16),
            pltpu.VMEM((6, 256, 256), F32),
            pltpu.VMEM((5, 256, 256), F32),
            pltpu.VMEM((6, 256, 128), F32),
            pltpu.VMEM((512, 512), BF16),
            pltpu.VMEM((4, 2, 256, 512), F32),
            pltpu.VMEM((3, 2, 256, 512), BF16),
            pltpu.VMEM((5, 256, 512), BF16),
            pltpu.VMEM((4, 2, 256, 512), BF16),
            pltpu.VMEM((4, 2, 64, 768), F32),
            pltpu.VMEM((4, 2, 64, 768), BF16),
            pltpu.VMEM((2, 64, 768), BF16),
            pltpu.VMEM((2, 64, 768), BF16),
            pltpu.VMEM((2, 2, 64, 768), BF16),
            pltpu.VMEM((64, 768), BF16),
            pltpu.VMEM((16, 256), F32),
            pltpu.VMEM((16, 256), F32),
            pltpu.VMEM((6, 512, 256), BF16),
            pltpu.VMEM((6, 512, 768), BF16),
            pltpu.VMEM((6, 768, 256), BF16),
            pltpu.VMEM((6, 768, 256), BF16),
            pltpu.VMEM((6, 128, 256), F32),
            pltpu.VMEM((6, 64, 256), F32),
            pltpu.VMEM((6, 64, 256), F32),
            pltpu.VMEM((6, 64, 256), F32),
            pltpu.VMEM((messages, 64, 256), HOP),
            pltpu.VMEM((messages, 64, 256), HOP),
            pltpu.VMEM((6, 128, 256), F32),
            pltpu.VMEM((64, 768), BF16),
            pltpu.VMEM((8, 64, 768), BF16),
            pltpu.VMEM((4, 2, 256, 512), BF16),
            pltpu.VMEM((2, 256, 512), F32),
            dma((9,)),
            dma((6,)),
            dma((5,)),
            dma((7,)),
            dma((3,)),
            dma((2, 2)),
            dma,
            dma,
            dma((messages,)),
            dma((messages,)),
            dma,
            dma,
            dma((7,)),
            dma((8,)),
            dma((5,)),
            dma((4, 2)),
        ],
        compiler_params=pltpu.CompilerParams(
            collective_id=0, has_side_effects=True, vmem_limit_bytes=60 * 1024 * 1024
        ),
    )(
        leaf_rhs[0],
        leaf_inverse[0],
        panels[0].reshape(768, 512),
        pattern,
        offsets,
        sep_inverse[0],
        sep_link[0],
        sep_rhs[0],
    )
    return x[None], sol[None]


def solution(mesh):
    in_specs = (
        P("leaf", "col", None),
        P("leaf", None, "col"),
        P("leaf", None, None, "col"),
        P("leaf", None),
        P("leaf", None),
        P("leaf", None, None, None),
        P("leaf", None, None, None),
        P("leaf", None, None, None),
    )
    out_specs = (P("leaf", "col", None), P("leaf", None, None, "col"))
    return jax.shard_map(on_device, mesh=mesh, in_specs=in_specs, out_specs=out_specs, check_vma=False)
```

```python
import functools

import jax
import jax.numpy as jnp
from jax import lax
from jax.experimental import pallas as pl
from jax.experimental.pallas import tpu as pltpu
from jax.sharding import PartitionSpec as P

MESH = pl.DeviceIdType.MESH
F32 = jnp.float32
BF16 = jnp.bfloat16
HOP = BF16
LEVELS = 6
MASKS = (1, 2, 6, 8, 16, 56)
PAIRS = tuple((k, j) for k in range(1, LEVELS) for j in range(k, LEVELS))


def dot_nn(a, b):
    return lax.dot_general(a, b, (((1,), (0,)), ((), ())), preferred_element_type=F32)


def dot_nt(a, b):
    return lax.dot_general(a, b, (((1,), (1,)), ((), ())), preferred_element_type=F32)


def halves(value):
    high = value.astype(BF16)
    return high, (value - high.astype(F32)).astype(BF16)


def wide(value):
    high, low = halves(value)
    return jnp.concatenate([high, low, high], axis=1)


def kernel(
    rhs, inv, pan, pat, off, sinv, slink, srhs, x_out, sol_out,
    rhs_v, inv_v, big, sinv_v, slink_v, srhs_v,
    bt, fp, fsnd, frx, cc, cb, prl, psum, prx, pon, meta, metarx, est,
    wf, wi, wg, rt, u, fs, bs, tsnd, trx, ball, solt, soth, sall, acc, xt,
    ld, f_ss, f_rs, p_ss, p_rs, prx_rs, m_ss, m_rs, t_ss, t_rs, b_ss, b_rs, s_ss, s_rs, g_ss, g_rs, o_s,
):
    leaf = lax.axis_index("leaf")
    c = lax.axis_index("col")
    q = lax.rem(leaf, 2)
    base = leaf - q
    c1, c2, c3 = lax.rem(c + 1, 4), lax.rem(c + 2, 4), lax.rem(c + 3, 4)
    rows = 512

    def remote(src, dst, ss, rs, to_leaf, to_col):
        return pltpu.make_async_remote_copy(
            src_ref=src, dst_ref=dst, send_sem=ss, recv_sem=rs,
            device_id=(to_leaf, to_col), device_id_type=MESH,
        )

    sent = []

    def on(cond, fn):
        pl.when(cond)(fn)

    def order(step):
        return jnp.where(c == 0, (2, 1, 3, 0)[step], 3 - step)

    load_rhs = pltpu.make_async_copy(rhs, rhs_v, ld.at[0])
    load_rhs.start()
    load_inv = []
    for step in range(4):
        r = jnp.maximum(order(step), 0)
        load_inv.append(
            pltpu.make_async_copy(inv.at[pl.ds(pl.multiple_of(r * rows, rows), rows)], inv_v.at[r], ld.at[1 + step])
        )
        on(step <= 3 - c, load_inv[step].start)
    load_pan = pltpu.make_async_copy(pan, big.at[c, pl.ds(0, 3)], ld.at[5])
    load_pan.start()
    load_sinv = pltpu.make_async_copy(sinv, sinv_v, ld.at[6])
    load_sinv.start()
    load_slink = pltpu.make_async_copy(slink, slink_v, ld.at[7])
    load_slink.start()
    load_srhs = pltpu.make_async_copy(
        srhs.at[:, :, pl.ds(pl.multiple_of(c * 128, 128), 128)], srhs_v, ld.at[8]
    )
    load_srhs.start()

    peers = [(leaf, c1), (leaf, c2), (leaf, c3)]
    peers += [(base + 1 - q, cc_) for cc_ in (c, c1, c2, c3)]
    peers += [(leaf ^ MASKS[k], c) for k in range(1, LEVELS)]
    barrier = pltpu.get_barrier_semaphore()
    for peer in peers:
        pl.semaphore_signal(barrier, inc=1, device_id=peer, device_id_type=MESH)

    for k in range(LEVELS):
        meta[pl.ds(k, 1), :] = jnp.full((1, 256), off[0, k].astype(F32), F32)
        meta[pl.ds(8 + k, 1), :] = jnp.full((1, 256), pat[0, k].astype(F32), F32)

    load_rhs.wait()
    bt[...] = rhs_v[...].T
    pl.semaphore_wait(barrier, len(peers))

    other = base + 1 - q
    send_meta = remote(meta, metarx, m_ss, m_rs, other, c)
    send_meta.start()

    def fmsg(sender, number, src, slot, to_col):
        return (c == sender, remote(src, frx.at[slot], f_ss.at[number], f_rs.at[slot], leaf, to_col))

    msgs = {
        "20A": fmsg(0, 0, fsnd.at[0, 0], 0, 1),
        "20B": fmsg(0, 1, fsnd.at[0, 1], 0, 3),
        "10A": fmsg(0, 2, fsnd.at[1, 0], 1, 1),
        "10B": fmsg(0, 3, fsnd.at[1, 1], 2, 1),
        "30A": fmsg(0, 4, fsnd.at[2, 0], 1, 3),
        "30B": fmsg(0, 5, fsnd.at[2, 1], 2, 3),
        "31A": fmsg(1, 0, fsnd.at[0, 0], 0, 0),
        "31B": fmsg(1, 1, fsnd.at[0, 1], 1, 0),
        "21B": fmsg(1, 2, fsnd.at[1, 1], 0, 2),
        "21A": fmsg(1, 3, fsnd.at[1, 0], 1, 2),
        "32A": fmsg(2, 0, fsnd.at[0, 0], 3, 3),
        "32B": fmsg(2, 1, fsnd.at[0, 1], 4, 3),
        "relay": fmsg(3, 0, frx.at[0], 2, 2),
    }
    now = {
        (0, 0): ("20A", "31A", "32A"),
        (0, 1): ("20B", "31B", "32B"),
        (1, 0): ("10A",),
        (1, 1): ("10B", "21B"),
    }
    for step in range(4):

        def block(step=step):
            load_inv[step].wait()
            r = order(step)
            for h in range(2):
                value = dot_nt(bt[pl.ds(h * 256, 256), :], inv_v[r])
                fp[step, h] = value
                if step < 3:
                    fsnd[step, h] = value.astype(BF16)
                for name in now.get((step, h), ()):
                    cond, copy = msgs[name]
                    on(cond, copy.start)

        on(step <= 3 - c, block)

    load_pan.wait()
    flows = []

    def flow(sender, number, r, p, to_col):
        copy = remote(big.at[r, p], big.at[r, p], g_ss.at[number], g_rs.at[r, p], leaf, to_col)
        flows.append((c == sender, copy))
        return flows[-1]

    def arrive(r, p):
        remote(big.at[r, p], big.at[r, p], g_ss.at[0], g_rs.at[r, p], leaf, c1).wait_recv()

    def start(*items):
        for cond, copy in items:
            on(cond, copy.start)

    def forward(cond, steps):
        def run():
            for r, p, (_, copy) in steps:
                arrive(r, p)
                copy.start()

        on(cond, run)

    start(*(flow(3, p, 3, p, 0) for p in range(3)), flow(3, 3, 3, 0, 2))
    start(*(flow(2, p, 2, p, 1) for p in range(3)), flow(2, 3, 2, 2, 3))
    start(flow(1, 0, 1, 0, 0))
    second = flow(3, 4, 3, 1, 2)

    load_sinv.wait()
    load_slink.wait()
    load_srhs.wait()
    highest = lax.Precision.HIGHEST

    def table(k, carry):
        ik = sinv_v[k]
        kk = jnp.minimum(k, LEVELS - 2)
        gk = lax.dot_general(
            slink_v[kk], ik, (((1,), (0,)), ((), ())), precision=highest, preferred_element_type=F32
        )
        ih, il = halves(ik)
        gh, gl = halves(gk)
        for at, (hi, lo) in ((0, (ih, il)), (256, (gh, gl))):
            wf[k, pl.ds(at, 256), pl.ds(0, 256)] = hi
            wf[k, pl.ds(at, 256), pl.ds(256, 256)] = hi
            wf[k, pl.ds(at, 256), pl.ds(512, 256)] = lo
        for ref, (hi, lo) in ((wi, (ih, il)), (wg, (gh, gl))):
            ref[k, pl.ds(0, 256), :] = hi
            ref[k, pl.ds(256, 256), :] = hi
            ref[k, pl.ds(512, 256), :] = lo
        rt[k] = srhs_v[k].T
        return carry

    lax.fori_loop(0, LEVELS, table, 0)

    send_meta.wait_recv()
    gap = (
        lax.broadcasted_iota(jnp.int32, (128, 256), 1) - lax.broadcasted_iota(jnp.int32, (128, 256), 0)
    ).astype(F32)
    for k in range(LEVELS):
        for part, ref in enumerate((meta, metarx)):
            spot = jnp.broadcast_to(ref[pl.ds(k, 1), :], (128, 256))
            keep = jnp.broadcast_to(ref[pl.ds(8 + k, 1), :], (128, 256))
            hot = jnp.where(gap == spot, keep, 0.0).astype(BF16)
            est[k, pl.ds(part * 256, 128), :] = hot
            est[k, pl.ds(part * 256 + 128, 128), :] = hot

    def product(r, p):
        return dot_nn(big[r, p], inv_v[r])

    def frecv(slot, from_col):
        remote(frx.at[slot], frx.at[slot], f_ss.at[0], f_rs.at[slot], leaf, from_col).wait_recv()

    def after0():
        for h, name in enumerate(("30A", "30B")):
            frecv(h, 1)
            fsnd[2, h] = (fp[2, h] + frx[h].astype(F32)).astype(BF16)
            msgs[name][1].start()
        for h in range(2):
            big[0, 3 + h] = fp[3, h].astype(BF16)

    def after1():
        frecv(0, 0)
        fsnd[1, 0] = (fp[1, 0] + frx[0].astype(F32)).astype(BF16)
        msgs["21A"][1].start()
        for h in range(2):
            frecv(1 + h, 0)
            big[1, 3 + h] = (fp[2, h] + frx[1 + h].astype(F32)).astype(BF16)

    def after2():
        frecv(1, 1)
        big[2, 3] = (fp[1, 0] + frx[1].astype(F32)).astype(BF16)
        frecv(0, 1)
        frecv(2, 3)
        big[2, 4] = (fp[1, 1] + frx[0].astype(F32) + frx[2].astype(F32)).astype(BF16)

    def after3():
        frecv(0, 0)
        msgs["relay"][1].start()
        second[1].start()
        for h in range(2):
            frecv(3 + h, 2)
            frecv(1 + h, 0)
            big[3, 3 + h] = (fp[0, h] + frx[1 + h].astype(F32) + frx[3 + h].astype(F32)).astype(BF16)

    for group, fn in enumerate((after0, after1, after2, after3)):
        on(c == group, fn)

    panels = big[c, pl.ds(0, 3)].reshape(768, 512)
    for h in range(2):
        share = dot_nt(big[c, 3 + h], panels).reshape(2, 2, 64, 768)
        cc[pl.ds(2 * h, 2)] = share
        cb[pl.ds(2 * h, 2)] = share.astype(BF16)
    relay_up = remote(cb.at[c2, 0], prl.at[0], p_ss.at[0], p_rs.at[0], leaf, c1)
    relay_down = remote(cb.at[c2, 1], prl.at[1], p_ss.at[1], p_rs.at[1], leaf, c3)
    direct_up = remote(cb.at[c1, 1], prx.at[q, 0], p_ss.at[2], prx_rs.at[q, 0], base + 1, c1)
    direct_down = remote(cb.at[c3, 0], prx.at[q, 1], p_ss.at[3], prx_rs.at[q, 1], base, c3)
    across = remote(cb.at[c, 1 - q], pon, p_ss.at[4], p_rs.at[2], other, c)
    sum_up = remote(psum.at[0], prx.at[q, 0], p_ss.at[5], prx_rs.at[q, 0], base, c1)
    sum_down = remote(psum.at[1], prx.at[q, 1], p_ss.at[6], prx_rs.at[q, 1], base + 1, c3)
    for copy in (relay_up, relay_down, direct_up, direct_down, across):
        copy.start()
    relay_up.wait_recv()
    psum[0] = (cc[c1, 0] + prl[0].astype(F32)).astype(BF16)
    sum_up.start()
    relay_down.wait_recv()
    psum[1] = (cc[c3, 1] + prl[1].astype(F32)).astype(BF16)
    sum_down.start()
    start(flow(3, 5, 3, 3, 0), flow(3, 6, 3, 4, 0), flow(3, 7, 3, 2, 2), flow(3, 8, 3, 3, 2), flow(3, 9, 3, 4, 2))
    start(flow(2, 4, 2, 3, 1), flow(2, 5, 2, 4, 1), flow(2, 6, 2, 3, 3), flow(2, 7, 2, 4, 3))
    start(flow(1, 1, 1, 1, 0), flow(1, 2, 1, 2, 0), flow(1, 3, 1, 3, 0), flow(1, 4, 1, 4, 0))
    forward(c == 3, [(2, 2, flow(3, 10, 2, 2, 0))])
    forward(c == 2, [(3, 0, flow(2, 8, 3, 0, 1)), (3, 1, flow(2, 9, 3, 1, 1))])
    forward(c == 1, [(2, 0, flow(1, 5, 2, 0, 0)), (2, 1, flow(1, 6, 2, 1, 0))])
    forward(c == 0, [(3, 2, flow(0, 0, 3, 2, 1))])
    across.wait_recv()

    def precv(p, d, from_col):
        remote(prx.at[p, d], prx.at[p, d], p_ss.at[0], prx_rs.at[p, d], base + p, from_col).wait_recv()

    for p in range(2):
        precv(p, 0, c3)
        precv(p, 1, c1)
    mine = cc[c, q] + prx[q, 0].astype(F32) + prx[q, 1].astype(F32)
    theirs = pon[...].astype(F32) + prx[1 - q, 0].astype(F32) + prx[1 - q, 1].astype(F32)
    mh, ml = halves(mine)
    th, tl = halves(theirs)
    for k in range(LEVELS):
        at = slice(k * 128, k * 128 + 128)
        left = jnp.concatenate([mh[:, at], ml[:, at], th[:, at], tl[:, at]], axis=1)
        u[k] = dot_nn(left, est[k])

    mine_rows = pl.ds(pl.multiple_of(q * 64, 64), 64)

    def tree(k, j):
        n = PAIRS.index((k, j))
        return remote(tsnd.at[n], trx.at[n], t_ss.at[n], t_rs.at[n], leaf ^ MASKS[k], c)

    def send(k, j):
        tsnd[PAIRS.index((k, j))] = u[j].astype(HOP)
        tree(k, j).start()

    def receive(k, j):
        tree(k, j).wait_recv()
        u[j] = u[j] + trx[PAIRS.index((k, j))].astype(F32)

    for k in range(LEVELS):
        if k > 0:
            receive(k, k)
        both = dot_nt(wide(rt[k, mine_rows, :] - u[k]), wf[k])
        if k + 1 < LEVELS:
            if k > 0:
                receive(k, k + 1)
            u[k + 1] = u[k + 1] + both[:, 256:]
            send(k + 1, k + 1)
            for j in range(k + 2, LEVELS):
                if k > 0:
                    receive(k, j)
                send(k + 1, j)
        fs[k] = dot_nn(wide(both[:, :256]), wi[k])
        if k < 5:
            acc[k] = product(c, k)
        if k == 3:
            forward(c == 3, [(2, 3, flow(3, 11, 2, 3, 0)), (2, 4, flow(3, 12, 2, 4, 0))])
            forward(c == 2, [(3, 3, flow(2, 10, 3, 3, 1))])
            forward(c == 0, [(3, 4, flow(0, 1, 3, 4, 1))])
    for k in reversed(range(LEVELS)):
        down = fs[k]
        if k + 1 < LEVELS:
            down = down - dot_nn(wide(bs[k + 1]), wg[k])
        bs[k] = down
        ball[k, mine_rows, :] = down

    swap = remote(ball.at[:, mine_rows, :], ball.at[:, mine_rows, :], b_ss, b_rs, other, c)
    slot = c * 2 + q
    for k in range(LEVELS):
        low = bs[k].astype(BF16)
        at = slice(k * 128, k * 128 + 128)
        sall[slot, :, at] = dot_nt(low, est[k, pl.ds(0, 128), :]).astype(BF16)
        soth[:, at] = dot_nt(low, est[k, pl.ds(256, 128), :]).astype(BF16)
    s_copies = [
        remote(sall.at[slot], sall.at[slot], s_ss.at[0], s_rs.at[slot], leaf, c1),
        remote(soth, sall.at[slot], s_ss.at[1], s_rs.at[slot], other, c1),
        remote(sall.at[slot], sall.at[slot], s_ss.at[2], s_rs.at[slot], leaf, c3),
        remote(soth, sall.at[slot], s_ss.at[3], s_rs.at[slot], other, c3),
        remote(soth, sall.at[slot], s_ss.at[4], s_rs.at[slot], other, c),
    ]
    for copy in s_copies:
        copy.start()
    swap.start()

    def srecv(at, from_leaf, from_col):
        remote(sall.at[at], sall.at[at], s_ss.at[0], s_rs.at[at], from_leaf, from_col).wait_recv()

    near, far = jnp.where(q == 0, c3, c1), jnp.where(q == 0, c1, c3)
    relays = []
    for p in range(2):
        at = near * 2 + p
        srecv(at, base + p, near)
        relays.append(remote(sall.at[at], sall.at[at], s_ss.at[5 + p], s_rs.at[at], leaf, far))
        relays[p].start()

    remote(ball.at[:, mine_rows, :], ball.at[:, mine_rows, :], b_ss, b_rs, other, c).wait_send()
    theirs_rows = pl.ds(pl.multiple_of((1 - q) * 64, 64), 64)
    remote(ball.at[:, theirs_rows, :], ball.at[:, theirs_rows, :], b_ss, b_rs, other, c).wait_recv()
    for k in range(LEVELS):
        solt[k] = ball[k].T
    put_sol = pltpu.make_async_copy(solt, sol_out, o_s.at[0])
    put_sol.start()

    for step in range(1, 4):

        def add(step=step):
            r = c + step
            for p in range(5):
                taken = (c == 0) & (r == 3) & (p in (2, 4))
                taken |= (c == 1) & (r == 2) & (p in (0, 1))
                taken |= (c == 2) & (r == 3) & (p in (0, 1, 3))
                on(jnp.logical_not(taken), functools.partial(arrive, r, p))
                acc[p] += product(r, p)

        on(c + step <= 3, add)

    srecv(c * 2 + 1 - q, other, c)
    for p in range(2):
        srecv(far * 2 + p, base + p, far)
    for p in range(2):
        srecv(c2 * 2 + p, leaf, near)
    weights = acc[pl.ds(0, 3)].reshape(768, 512).astype(BF16)
    for h in range(2):
        taken = sall[pl.ds(4 * h, 4)].reshape(256, 768)
        xt[:, pl.ds(h * 256, 256)] = (acc[3 + h] - dot_nn(taken, weights)).T.astype(BF16)
    put_x = pltpu.make_async_copy(xt, x_out, o_s.at[1])
    put_x.start()

    for copy in (send_meta, relay_up, relay_down, direct_up, direct_down, across, sum_up, sum_down, *s_copies, *relays):
        copy.wait_send()
    for k, j in PAIRS:
        tree(k, j).wait_send()
    for cond, copy in (*msgs.values(), *flows):
        on(cond, copy.wait_send)
    put_sol.wait()
    put_x.wait()


def on_device(leaf_rhs, leaf_inverse, panels, pattern, offsets, sep_inverse, sep_link, sep_rhs):
    anywhere = pl.BlockSpec(memory_space=pl.ANY)
    hbm = pl.BlockSpec(memory_space=pltpu.HBM)
    scalars = pl.BlockSpec(memory_space=pltpu.SMEM)
    dma = pltpu.SemaphoreType.DMA
    messages = len(PAIRS)
    x, sol = pl.pallas_call(
        kernel,
        out_shape=(jax.ShapeDtypeStruct((512, 512), BF16), jax.ShapeDtypeStruct((6, 256, 128), F32)),
        in_specs=[hbm, hbm, hbm, scalars, scalars, hbm, hbm, hbm],
        out_specs=(anywhere, anywhere),
        scratch_shapes=[
            pltpu.VMEM((512, 512), BF16),
            pltpu.VMEM((4, 512, 512), BF16),
            pltpu.VMEM((4, 5, 256, 512), BF16),
            pltpu.VMEM((6, 256, 256), F32),
            pltpu.VMEM((5, 256, 256), F32),
            pltpu.VMEM((6, 256, 128), F32),
            pltpu.VMEM((512, 512), BF16),
            pltpu.VMEM((4, 2, 256, 512), F32),
            pltpu.VMEM((3, 2, 256, 512), BF16),
            pltpu.VMEM((5, 256, 512), BF16),
            pltpu.VMEM((4, 2, 64, 768), F32),
            pltpu.VMEM((4, 2, 64, 768), BF16),
            pltpu.VMEM((2, 64, 768), BF16),
            pltpu.VMEM((2, 64, 768), BF16),
            pltpu.VMEM((2, 2, 64, 768), BF16),
            pltpu.VMEM((64, 768), BF16),
            pltpu.VMEM((16, 256), F32),
            pltpu.VMEM((16, 256), F32),
            pltpu.VMEM((6, 512, 256), BF16),
            pltpu.VMEM((6, 512, 768), BF16),
            pltpu.VMEM((6, 768, 256), BF16),
            pltpu.VMEM((6, 768, 256), BF16),
            pltpu.VMEM((6, 128, 256), F32),
            pltpu.VMEM((6, 64, 256), F32),
            pltpu.VMEM((6, 64, 256), F32),
            pltpu.VMEM((6, 64, 256), F32),
            pltpu.VMEM((messages, 64, 256), HOP),
            pltpu.VMEM((messages, 64, 256), HOP),
            pltpu.VMEM((6, 128, 256), F32),
            pltpu.VMEM((6, 256, 128), F32),
            pltpu.VMEM((64, 768), BF16),
            pltpu.VMEM((8, 64, 768), BF16),
            pltpu.VMEM((5, 256, 512), F32),
            pltpu.VMEM((512, 512), BF16),
            dma((9,)),
            dma((6,)),
            dma((5,)),
            dma((7,)),
            dma((3,)),
            dma((2, 2)),
            dma,
            dma,
            dma((messages,)),
            dma((messages,)),
            dma,
            dma,
            dma((7,)),
            dma((8,)),
            dma((13,)),
            dma((4, 5)),
            dma((2,)),
        ],
        compiler_params=pltpu.CompilerParams(
            collective_id=0, has_side_effects=True, vmem_limit_bytes=46 * 1024 * 1024
        ),
    )(
        leaf_rhs[0],
        leaf_inverse[0],
        panels[0].reshape(3, 256, 512),
        pattern,
        offsets,
        sep_inverse[0],
        sep_link[0],
        sep_rhs[0],
    )
    return x[None], sol[None]


def solution(mesh):
    in_specs = (
        P("leaf", "col", None),
        P("leaf", None, "col"),
        P("leaf", None, None, "col"),
        P("leaf", None),
        P("leaf", None),
        P("leaf", None, None, None),
        P("leaf", None, None, None),
        P("leaf", None, None, None),
    )
    out_specs = (P("leaf", "col", None), P("leaf", None, None, "col"))
    return jax.shard_map(on_device, mesh=mesh, in_specs=in_specs, out_specs=out_specs, check_vma=False)
```

```python
import functools

import jax
import jax.numpy as jnp
from jax import lax
from jax.experimental import pallas as pl
from jax.experimental.pallas import tpu as pltpu
from jax.sharding import PartitionSpec as P

MESH = pl.DeviceIdType.MESH
F32 = jnp.float32
BF16 = jnp.bfloat16
HOP = BF16
LEVELS = 6
MASKS = (1, 2, 6, 8, 16, 56)
PAIRS = tuple((k, j) for k in range(1, LEVELS) for j in range(k, LEVELS))


def dot_nn(a, b):
    return lax.dot_general(a, b, (((1,), (0,)), ((), ())), preferred_element_type=F32)


def dot_nt(a, b):
    return lax.dot_general(a, b, (((1,), (1,)), ((), ())), preferred_element_type=F32)


def halves(value):
    high = value.astype(BF16)
    return high, (value - high.astype(F32)).astype(BF16)


def wide(value):
    high, low = halves(value)
    return jnp.concatenate([high, low, high], axis=1)


def kernel(
    rhs, inv, pan, pat, off, sinv, slink, srhs, x_out, sol_out,
    rhs_v, inv_v, big, sinv_v, slink_v, srhs_v,
    bt, fp, fsnd, frx, cc, cb, prl, psum, prx, pon, meta, metarx, est,
    wf, wi, wg, rt, u, fs, bs, tsnd, trx, ball, solt, soth, sall, acc, xt,
    ld, f_ss, f_rs, p_ss, p_rs, prx_rs, m_ss, m_rs, t_ss, t_rs, b_ss, b_rs, s_ss, s_rs, g_ss, g_rs, o_s,
):
    leaf = lax.axis_index("leaf")
    c = lax.axis_index("col")
    q = lax.rem(leaf, 2)
    base = leaf - q
    c1, c2, c3 = lax.rem(c + 1, 4), lax.rem(c + 2, 4), lax.rem(c + 3, 4)
    rows = 512

    def remote(src, dst, ss, rs, to_leaf, to_col):
        return pltpu.make_async_remote_copy(
            src_ref=src, dst_ref=dst, send_sem=ss, recv_sem=rs,
            device_id=(to_leaf, to_col), device_id_type=MESH,
        )

    sent = []

    def on(cond, fn):
        pl.when(cond)(fn)

    def order(step):
        return jnp.where(c == 0, (2, 1, 3, 0)[step], 3 - step)

    load_rhs = pltpu.make_async_copy(rhs, rhs_v, ld.at[0])
    load_rhs.start()
    load_inv = []
    for step in range(4):
        r = jnp.maximum(order(step), 0)
        load_inv.append(
            pltpu.make_async_copy(inv.at[pl.ds(pl.multiple_of(r * rows, rows), rows)], inv_v.at[r], ld.at[1 + step])
        )
        on(step <= 3 - c, load_inv[step].start)
    peers = [(leaf, c1), (leaf, c2), (leaf, c3)]
    peers += [(base + 1 - q, cc_) for cc_ in (c, c1, c2, c3)]
    peers += [(leaf ^ MASKS[k], c) for k in range(1, LEVELS)]
    barrier = pltpu.get_barrier_semaphore()
    for peer in peers:
        pl.semaphore_signal(barrier, inc=1, device_id=peer, device_id_type=MESH)

    for k in range(LEVELS):
        meta[pl.ds(k, 1), :] = jnp.full((1, 256), off[0, k].astype(F32), F32)
        meta[pl.ds(8 + k, 1), :] = jnp.full((1, 256), pat[0, k].astype(F32), F32)

    load_rhs.wait()
    bt[...] = rhs_v[...].T
    pl.semaphore_wait(barrier, len(peers))

    other = base + 1 - q
    send_meta = remote(meta, metarx, m_ss, m_rs, other, c)
    send_meta.start()

    def fmsg(sender, number, src, slot, to_col):
        return (c == sender, remote(src, frx.at[slot], f_ss.at[number], f_rs.at[slot], leaf, to_col))

    msgs = {}

    def messages(sender, to_col, items):
        for step, n, slot in items:
            number = sum(1 for key in msgs if key[0] == sender)
            msgs[sender, to_col, step, n] = fmsg(sender, number, fsnd.at[step, n], slot, to_col)

    messages(0, 1, [(0, 0, 0), (0, 1, 1), (1, 0, 2), (1, 1, 3), (1, 2, 4), (1, 3, 5)])
    messages(0, 3, [(0, 2, 0), (0, 3, 1), (2, 2, 4), (2, 3, 5), (2, 0, 2), (2, 1, 3)])
    messages(1, 0, [(0, 0, 0), (0, 1, 1)])
    messages(1, 2, [(0, 2, 0), (0, 3, 1), (1, 2, 4), (1, 3, 5), (1, 0, 2), (1, 1, 3)])
    messages(2, 3, [(0, 0, 6), (0, 1, 7), (0, 2, 8), (0, 3, 9)])
    msgs[3, 2, 9, 0] = fmsg(3, 0, frx.at[0], 6, 2)
    msgs[3, 2, 9, 1] = fmsg(3, 1, frx.at[1], 7, 2)
    later = {(0, 3, 2, 0), (0, 3, 2, 1), (1, 2, 1, 0), (1, 2, 1, 1), (2, 3, 0, 2), (2, 3, 0, 3)}
    for step in range(4):

        def block(step=step):
            load_inv[step].wait()
            r = order(step)
            for h in range(2):
                value = dot_nt(bt[pl.ds(h * 256, 256), :], inv_v[r]).reshape(2, 128, 512)
                fp[step, pl.ds(2 * h, 2)] = value
                if step < 3:
                    fsnd[step, pl.ds(2 * h, 2)] = value.astype(BF16)
                for key, (cond, copy) in msgs.items():
                    if key[2] == step and key[3] // 2 == h and key not in later:
                        on(cond, copy.start)

        on(step <= 3 - c, block)
        if step == 0:
            load_pan = pltpu.make_async_copy(pan, big.at[c, pl.ds(0, 3)], ld.at[5])
            load_pan.start()
            load_sinv = pltpu.make_async_copy(sinv, sinv_v, ld.at[6])
            load_sinv.start()
            load_slink = pltpu.make_async_copy(slink, slink_v, ld.at[7])
            load_slink.start()
            load_srhs = pltpu.make_async_copy(
                srhs.at[:, :, pl.ds(pl.multiple_of(c * 128, 128), 128)], srhs_v, ld.at[8]
            )
            load_srhs.start()

    load_pan.wait()
    flows = []

    def flow(sender, number, r, p, to_col):
        copy = remote(big.at[r, p], big.at[r, p], g_ss.at[number], g_rs.at[r, p], leaf, to_col)
        flows.append((c == sender, copy))
        return flows[-1]

    def arrive(r, p):
        remote(big.at[r, p], big.at[r, p], g_ss.at[0], g_rs.at[r, p], leaf, c1).wait_recv()

    def start(*items):
        for cond, copy in items:
            on(cond, copy.start)

    def forward(cond, steps):
        def run():
            for r, p, (_, copy) in steps:
                arrive(r, p)
                copy.start()

        on(cond, run)

    start(*(flow(3, p, 3, p, 0) for p in range(3)), flow(3, 3, 3, 0, 2))
    start(*(flow(2, p, 2, p, 1) for p in range(3)), flow(2, 3, 2, 2, 3))
    start(flow(1, 0, 1, 0, 0), flow(1, 1, 1, 1, 0))
    second = flow(3, 4, 3, 1, 2)

    load_sinv.wait()
    load_slink.wait()
    load_srhs.wait()
    highest = lax.Precision.HIGHEST

    def table(k, carry):
        ik = sinv_v[k]
        kk = jnp.minimum(k, LEVELS - 2)
        gk = lax.dot_general(
            slink_v[kk], ik, (((1,), (0,)), ((), ())), precision=highest, preferred_element_type=F32
        )
        ih, il = halves(ik)
        gh, gl = halves(gk)
        for at, (hi, lo) in ((0, (ih, il)), (256, (gh, gl))):
            wf[k, pl.ds(at, 256), pl.ds(0, 256)] = hi
            wf[k, pl.ds(at, 256), pl.ds(256, 256)] = hi
            wf[k, pl.ds(at, 256), pl.ds(512, 256)] = lo
        for ref, (hi, lo) in ((wi, (ih, il)), (wg, (gh, gl))):
            ref[k, pl.ds(0, 256), :] = hi
            ref[k, pl.ds(256, 256), :] = hi
            ref[k, pl.ds(512, 256), :] = lo
        rt[k] = srhs_v[k].T
        return carry

    lax.fori_loop(0, LEVELS, table, 0)

    send_meta.wait_recv()
    gap = (
        lax.broadcasted_iota(jnp.int32, (128, 256), 1) - lax.broadcasted_iota(jnp.int32, (128, 256), 0)
    ).astype(F32)
    for k in range(LEVELS):
        for part, ref in enumerate((meta, metarx)):
            spot = jnp.broadcast_to(ref[pl.ds(k, 1), :], (128, 256))
            keep = jnp.broadcast_to(ref[pl.ds(8 + k, 1), :], (128, 256))
            hot = jnp.where(gap == spot, keep, 0.0).astype(BF16)
            est[k, pl.ds(part * 256, 128), :] = hot
            est[k, pl.ds(part * 256 + 128, 128), :] = hot

    def product(r, p):
        return dot_nn(big[r, p], inv_v[r])

    def frecv(slot, from_col):
        remote(frx.at[slot], frx.at[slot], f_ss.at[0], f_rs.at[slot], leaf, from_col).wait_recv()

    def got(slot, from_col):
        frecv(slot, from_col)
        return frx[slot].astype(F32)

    def add_and_send(key, slot, from_col):
        _, _, step, n = key
        fsnd[step, n] = (fp[step, n] + got(slot, from_col)).astype(BF16)
        msgs[key][1].start()

    def solved(r, n, value):
        big[r, 3 + n // 2, pl.ds(n % 2 * 128, 128), :] = value.astype(BF16)

    def after0():
        add_and_send((0, 3, 2, 0), 0, 1)
        add_and_send((0, 3, 2, 1), 1, 1)
        for n in range(4):
            solved(0, n, fp[3, n])

    def after1():
        add_and_send((1, 2, 1, 0), 0, 0)
        add_and_send((1, 2, 1, 1), 1, 0)
        for n in range(4):
            solved(1, n, fp[2, n] + got(2 + n, 0))

    def after2():
        add_and_send((2, 3, 0, 2), 0, 1)
        add_and_send((2, 3, 0, 3), 1, 1)
        for n in (2, 3):
            solved(2, n, fp[1, n] + got(2 + n, 1) + got(4 + n, 3))
        for n in (0, 1):
            solved(2, n, fp[1, n] + got(2 + n, 1))

    def after3():
        for n in range(2):
            frecv(n, 0)
            msgs[3, 2, 9, n][1].start()
        second[1].start()
        for n in (2, 3, 0, 1):
            solved(3, n, fp[0, n] + got(6 + n, 2) + got(2 + n, 0))

    for group, fn in enumerate((after0, after1, after2, after3)):
        on(c == group, fn)

    panels = big[c, pl.ds(0, 3)].reshape(768, 512)

    def share(j):
        rows_j = pl.ds(pl.multiple_of(lax.rem(j, 2) * 128, 128), 128)
        value = dot_nt(big[c, 3 + lax.div(j, 2), rows_j, :], panels).reshape(2, 64, 768)
        cc[j] = value
        cb[j] = value.astype(BF16)

    relay_up = remote(cb.at[c2, 0], prl.at[0], p_ss.at[0], p_rs.at[0], leaf, c1)
    relay_down = remote(cb.at[c2, 1], prl.at[1], p_ss.at[1], p_rs.at[1], leaf, c3)
    direct_up = remote(cb.at[c1, 1], prx.at[q, 0], p_ss.at[2], prx_rs.at[q, 0], base + 1, c1)
    direct_down = remote(cb.at[c3, 0], prx.at[q, 1], p_ss.at[3], prx_rs.at[q, 1], base, c3)
    across = remote(cb.at[c, 1 - q], pon, p_ss.at[4], p_rs.at[2], other, c)
    sum_up = remote(psum.at[0], prx.at[q, 0], p_ss.at[5], prx_rs.at[q, 0], base, c1)
    sum_down = remote(psum.at[1], prx.at[q, 1], p_ss.at[6], prx_rs.at[q, 1], base + 1, c3)
    share(c2)
    relay_up.start()
    relay_down.start()
    share(c1)
    direct_up.start()
    share(c3)
    direct_down.start()
    share(c)
    across.start()
    relay_up.wait_recv()
    psum[0] = (cc[c1, 0] + prl[0].astype(F32)).astype(BF16)
    sum_up.start()
    relay_down.wait_recv()
    psum[1] = (cc[c3, 1] + prl[1].astype(F32)).astype(BF16)
    sum_down.start()
    start(flow(3, 5, 3, 3, 0), flow(3, 6, 3, 4, 0), flow(3, 7, 3, 2, 2), flow(3, 8, 3, 3, 2), flow(3, 9, 3, 4, 2))
    start(flow(2, 4, 2, 3, 1), flow(2, 5, 2, 4, 1), flow(2, 6, 2, 3, 3), flow(2, 7, 2, 4, 3))
    start(flow(1, 2, 1, 2, 0), flow(1, 3, 1, 3, 0), flow(1, 4, 1, 4, 0))
    forward(c == 3, [(2, 2, flow(3, 10, 2, 2, 0))])
    forward(c == 2, [(3, 0, flow(2, 8, 3, 0, 1)), (3, 1, flow(2, 9, 3, 1, 1))])
    forward(c == 1, [(2, 0, flow(1, 5, 2, 0, 0)), (2, 1, flow(1, 6, 2, 1, 0))])
    forward(c == 0, [(3, 2, flow(0, 0, 3, 2, 1))])
    across.wait_recv()

    def precv(p, d, from_col):
        remote(prx.at[p, d], prx.at[p, d], p_ss.at[0], prx_rs.at[p, d], base + p, from_col).wait_recv()

    for p in range(2):
        precv(p, 0, c3)
        precv(p, 1, c1)
    mine = cc[c, q] + prx[q, 0].astype(F32) + prx[q, 1].astype(F32)
    theirs = pon[...].astype(F32) + prx[1 - q, 0].astype(F32) + prx[1 - q, 1].astype(F32)
    mh, ml = halves(mine)
    th, tl = halves(theirs)
    for k in range(LEVELS):
        at = slice(k * 128, k * 128 + 128)
        left = jnp.concatenate([mh[:, at], ml[:, at], th[:, at], tl[:, at]], axis=1)
        u[k] = dot_nn(left, est[k])

    mine_rows = pl.ds(pl.multiple_of(q * 64, 64), 64)

    def tree(k, j):
        n = PAIRS.index((k, j))
        return remote(tsnd.at[n], trx.at[n], t_ss.at[n], t_rs.at[n], leaf ^ MASKS[k], c)

    def send(k, j):
        tsnd[PAIRS.index((k, j))] = u[j].astype(HOP)
        tree(k, j).start()

    def receive(k, j):
        tree(k, j).wait_recv()
        u[j] = u[j] + trx[PAIRS.index((k, j))].astype(F32)

    for k in range(LEVELS):
        if k > 0:
            receive(k, k)
        both = dot_nt(wide(rt[k, mine_rows, :] - u[k]), wf[k])
        if k + 1 < LEVELS:
            if k > 0:
                receive(k, k + 1)
            u[k + 1] = u[k + 1] + both[:, 256:]
            send(k + 1, k + 1)
            for j in range(k + 2, LEVELS):
                if k > 0:
                    receive(k, j)
                send(k + 1, j)
        fs[k] = dot_nn(wide(both[:, :256]), wi[k])
        if k < 5:
            acc[k] = product(c, k)
        if k == 3:
            forward(c == 3, [(2, 3, flow(3, 11, 2, 3, 0)), (2, 4, flow(3, 12, 2, 4, 0))])
            forward(c == 2, [(3, 3, flow(2, 10, 3, 3, 1))])
            forward(c == 0, [(3, 4, flow(0, 1, 3, 4, 1))])
    for k in reversed(range(LEVELS)):
        down = fs[k]
        if k + 1 < LEVELS:
            down = down - dot_nn(wide(bs[k + 1]), wg[k])
        bs[k] = down
        ball[k, mine_rows, :] = down

    swap = remote(ball.at[:, mine_rows, :], ball.at[:, mine_rows, :], b_ss, b_rs, other, c)
    slot = c * 2 + q
    for k in range(LEVELS):
        low = bs[k].astype(BF16)
        at = slice(k * 128, k * 128 + 128)
        sall[slot, :, at] = dot_nt(low, est[k, pl.ds(0, 128), :]).astype(BF16)
        soth[:, at] = dot_nt(low, est[k, pl.ds(256, 128), :]).astype(BF16)
    s_copies = [
        remote(sall.at[slot], sall.at[slot], s_ss.at[0], s_rs.at[slot], leaf, c1),
        remote(soth, sall.at[slot], s_ss.at[1], s_rs.at[slot], other, c1),
        remote(sall.at[slot], sall.at[slot], s_ss.at[2], s_rs.at[slot], leaf, c3),
        remote(soth, sall.at[slot], s_ss.at[3], s_rs.at[slot], other, c3),
        remote(soth, sall.at[slot], s_ss.at[4], s_rs.at[slot], other, c),
    ]
    for copy in s_copies:
        copy.start()
    swap.start()

    def srecv(at, from_leaf, from_col):
        remote(sall.at[at], sall.at[at], s_ss.at[0], s_rs.at[at], from_leaf, from_col).wait_recv()

    near, far = jnp.where(q == 0, c3, c1), jnp.where(q == 0, c1, c3)
    relays = []
    for p in range(2):
        at = near * 2 + p
        srecv(at, base + p, near)
        relays.append(remote(sall.at[at], sall.at[at], s_ss.at[5 + p], s_rs.at[at], leaf, far))
        relays[p].start()

    remote(ball.at[:, mine_rows, :], ball.at[:, mine_rows, :], b_ss, b_rs, other, c).wait_send()
    theirs_rows = pl.ds(pl.multiple_of((1 - q) * 64, 64), 64)
    remote(ball.at[:, theirs_rows, :], ball.at[:, theirs_rows, :], b_ss, b_rs, other, c).wait_recv()
    for k in range(LEVELS):
        solt[k] = ball[k].T
    put_sol = pltpu.make_async_copy(solt, sol_out, o_s.at[0])
    put_sol.start()

    for step in range(1, 4):

        def add(step=step):
            r = c + step
            for p in range(5):
                taken = (c == 0) & (r == 3) & (p in (2, 4))
                taken |= (c == 1) & (r == 2) & (p in (0, 1))
                taken |= (c == 2) & (r == 3) & (p in (0, 1, 3))
                on(jnp.logical_not(taken), functools.partial(arrive, r, p))
                acc[p] += product(r, p)

        on(c + step <= 3, add)

    weights = acc[pl.ds(0, 3)].reshape(768, 512).astype(BF16)
    puts = []

    def final(y):
        taken = sall[pl.ds(2 * y, 2)].reshape(128, 768)
        rows_y = pl.ds(pl.multiple_of(lax.rem(y, 2) * 128, 128), 128)
        to = pl.ds(pl.multiple_of(y * 128, 128), 128)
        value = acc[3 + lax.div(y, 2), rows_y, :] - dot_nn(taken, weights)
        xt[:, to] = value.T.astype(BF16)
        puts.append(pltpu.make_async_copy(xt.at[:, to], x_out.at[:, to], o_s.at[1 + len(puts)]))
        puts[-1].start()

    srecv(c * 2 + 1 - q, other, c)
    final(c)
    final(near)
    for p in range(2):
        srecv(far * 2 + p, base + p, far)
    final(far)
    for p in range(2):
        srecv(c2 * 2 + p, leaf, near)
    final(c2)

    for copy in (send_meta, relay_up, relay_down, direct_up, direct_down, across, sum_up, sum_down, *s_copies, *relays):
        copy.wait_send()
    for k, j in PAIRS:
        tree(k, j).wait_send()
    for cond, copy in (*msgs.values(), *flows):
        on(cond, copy.wait_send)
    put_sol.wait()
    for put in puts:
        put.wait()


def on_device(leaf_rhs, leaf_inverse, panels, pattern, offsets, sep_inverse, sep_link, sep_rhs):
    anywhere = pl.BlockSpec(memory_space=pl.ANY)
    in_hbm = functools.partial(pltpu.with_memory_space_constraint, memory_space=pltpu.HBM)
    hbm = pl.BlockSpec(memory_space=pltpu.HBM)
    scalars = pl.BlockSpec(memory_space=pltpu.SMEM)
    dma = pltpu.SemaphoreType.DMA
    messages = len(PAIRS)
    x, sol = pl.pallas_call(
        kernel,
        out_shape=(jax.ShapeDtypeStruct((512, 512), BF16), jax.ShapeDtypeStruct((6, 256, 128), F32)),
        in_specs=[hbm, hbm, hbm, scalars, scalars, hbm, hbm, hbm],
        out_specs=(anywhere, anywhere),
        scratch_shapes=[
            pltpu.VMEM((512, 512), BF16),
            pltpu.VMEM((4, 512, 512), BF16),
            pltpu.VMEM((4, 5, 256, 512), BF16),
            pltpu.VMEM((6, 256, 256), F32),
            pltpu.VMEM((5, 256, 256), F32),
            pltpu.VMEM((6, 256, 128), F32),
            pltpu.VMEM((512, 512), BF16),
            pltpu.VMEM((4, 4, 128, 512), F32),
            pltpu.VMEM((3, 4, 128, 512), BF16),
            pltpu.VMEM((10, 128, 512), BF16),
            pltpu.VMEM((4, 2, 64, 768), F32),
            pltpu.VMEM((4, 2, 64, 768), BF16),
            pltpu.VMEM((2, 64, 768), BF16),
            pltpu.VMEM((2, 64, 768), BF16),
            pltpu.VMEM((2, 2, 64, 768), BF16),
            pltpu.VMEM((64, 768), BF16),
            pltpu.VMEM((16, 256), F32),
            pltpu.VMEM((16, 256), F32),
            pltpu.VMEM((6, 512, 256), BF16),
            pltpu.VMEM((6, 512, 768), BF16),
            pltpu.VMEM((6, 768, 256), BF16),
            pltpu.VMEM((6, 768, 256), BF16),
            pltpu.VMEM((6, 128, 256), F32),
            pltpu.VMEM((6, 64, 256), F32),
            pltpu.VMEM((6, 64, 256), F32),
            pltpu.VMEM((6, 64, 256), F32),
            pltpu.VMEM((messages, 64, 256), HOP),
            pltpu.VMEM((messages, 64, 256), HOP),
            pltpu.VMEM((6, 128, 256), F32),
            pltpu.VMEM((6, 256, 128), F32),
            pltpu.VMEM((64, 768), BF16),
            pltpu.VMEM((8, 64, 768), BF16),
            pltpu.VMEM((5, 256, 512), F32),
            pltpu.VMEM((512, 512), BF16),
            dma((9,)),
            dma((12,)),
            dma((10,)),
            dma((7,)),
            dma((3,)),
            dma((2, 2)),
            dma,
            dma,
            dma((messages,)),
            dma((messages,)),
            dma,
            dma,
            dma((7,)),
            dma((8,)),
            dma((13,)),
            dma((4, 5)),
            dma((5,)),
        ],
        compiler_params=pltpu.CompilerParams(
            collective_id=0, has_side_effects=True, vmem_limit_bytes=46 * 1024 * 1024
        ),
    )(
        in_hbm(leaf_rhs[0]),
        in_hbm(leaf_inverse[0]),
        in_hbm(panels[0].reshape(3, 256, 512)),
        in_hbm(pattern),
        in_hbm(offsets),
        in_hbm(sep_inverse[0]),
        in_hbm(sep_link[0]),
        in_hbm(sep_rhs[0]),
    )
    return x[None], sol[None]


def solution(mesh):
    in_specs = (
        P("leaf", "col", None),
        P("leaf", None, "col"),
        P("leaf", None, None, "col"),
        P("leaf", None),
        P("leaf", None),
        P("leaf", None, None, None),
        P("leaf", None, None, None),
        P("leaf", None, None, None),
    )
    out_specs = (P("leaf", "col", None), P("leaf", None, None, "col"))
    return jax.shard_map(on_device, mesh=mesh, in_specs=in_specs, out_specs=out_specs, check_vma=False)
```

```python
import functools

import jax
import jax.numpy as jnp
from jax import lax
from jax.experimental import pallas as pl
from jax.experimental.pallas import tpu as pltpu
from jax.sharding import PartitionSpec as P

MESH = pl.DeviceIdType.MESH
F32 = jnp.float32
BF16 = jnp.bfloat16
HOP = BF16
LEVELS = 6
MASKS = (1, 2, 6, 8, 16, 56)
PAIRS = tuple((k, j) for k in range(1, LEVELS) for j in range(k, LEVELS))


def dot_nn(a, b):
    return lax.dot_general(a, b, (((1,), (0,)), ((), ())), preferred_element_type=F32)


def dot_nt(a, b):
    return lax.dot_general(a, b, (((1,), (1,)), ((), ())), preferred_element_type=F32)


def halves(value):
    high = value.astype(BF16)
    return high, (value - high.astype(F32)).astype(BF16)


def wide(value):
    high, low = halves(value)
    return jnp.concatenate([high, low, high], axis=1)


def kernel(
    rhs, inv, pan, pat, off, sinv, slink, srhs, x_out, sol_out,
    rhs_v, inv_v, big, sinv_v, slink_v, srhs_v,
    bt, fp, fsnd, frx, cc, cb, prl, psum, prx, pon, meta, metarx, est,
    wf, wi, wg, rt, u, fs, bs, tsnd, trx, ball, solt, soth, sall, acc, xt,
    ld, f_ss, f_rs, p_ss, p_rs, prx_rs, m_ss, m_rs, t_ss, t_rs, b_ss, b_rs, s_ss, s_rs, g_ss, g_rs, o_s,
):
    leaf = lax.axis_index("leaf")
    c = lax.axis_index("col")
    q = lax.rem(leaf, 2)
    base = leaf - q
    c1, c2, c3 = lax.rem(c + 1, 4), lax.rem(c + 2, 4), lax.rem(c + 3, 4)
    rows = 512

    def remote(src, dst, ss, rs, to_leaf, to_col):
        return pltpu.make_async_remote_copy(
            src_ref=src, dst_ref=dst, send_sem=ss, recv_sem=rs,
            device_id=(to_leaf, to_col), device_id_type=MESH,
        )

    sent = []

    def on(cond, fn):
        pl.when(cond)(fn)

    def order(step):
        return jnp.where(c == 0, (2, 1, 3, 0)[step], 3 - step)

    load_rhs = pltpu.make_async_copy(rhs, rhs_v, ld.at[0])
    load_rhs.start()
    load_inv = []
    for step in range(4):
        r = jnp.maximum(order(step), 0)
        load_inv.append(
            pltpu.make_async_copy(inv.at[pl.ds(pl.multiple_of(r * rows, rows), rows)], inv_v.at[r], ld.at[1 + step])
        )
        on(step <= 3 - c, load_inv[step].start)
    peers = [(leaf, c1), (leaf, c2), (leaf, c3)]
    peers += [(base + 1 - q, cc_) for cc_ in (c, c1, c2, c3)]
    peers += [(leaf ^ MASKS[k], c) for k in range(1, LEVELS)]
    barrier = pltpu.get_barrier_semaphore()
    for peer in peers:
        pl.semaphore_signal(barrier, inc=1, device_id=peer, device_id_type=MESH)

    for k in range(LEVELS):
        meta[pl.ds(k, 1), :] = jnp.full((1, 256), off[0, k].astype(F32), F32)
        meta[pl.ds(8 + k, 1), :] = jnp.full((1, 256), pat[0, k].astype(F32), F32)

    load_rhs.wait()
    bt[...] = rhs_v[...].T
    pl.semaphore_wait(barrier, len(peers))

    other = base + 1 - q
    send_meta = remote(meta, metarx, m_ss, m_rs, other, c)
    send_meta.start()

    def fmsg(sender, number, src, slot, to_col):
        return (c == sender, remote(src, frx.at[slot], f_ss.at[number], f_rs.at[slot], leaf, to_col))

    msgs = {}

    def messages(sender, to_col, items):
        for step, n, slot in items:
            number = sum(1 for key in msgs if key[0] == sender)
            msgs[sender, to_col, step, n] = fmsg(sender, number, fsnd.at[step, n], slot, to_col)

    messages(0, 1, [(0, 0, 0), (0, 1, 1), (1, 0, 2), (1, 1, 3), (1, 2, 4), (1, 3, 5)])
    messages(0, 3, [(0, 2, 0), (0, 3, 1), (2, 2, 4), (2, 3, 5), (2, 0, 2), (2, 1, 3)])
    messages(1, 0, [(0, 0, 0), (0, 1, 1)])
    messages(1, 2, [(0, 2, 0), (0, 3, 1), (1, 2, 4), (1, 3, 5), (1, 0, 2), (1, 1, 3)])
    messages(2, 3, [(0, 0, 6), (0, 1, 7), (0, 2, 8), (0, 3, 9)])
    msgs[3, 2, 9, 0] = fmsg(3, 0, frx.at[0], 6, 2)
    msgs[3, 2, 9, 1] = fmsg(3, 1, frx.at[1], 7, 2)
    later = {(0, 3, 2, 0), (0, 3, 2, 1), (1, 2, 1, 0), (1, 2, 1, 1), (2, 3, 0, 2), (2, 3, 0, 3)}
    for step in range(4):

        def block(step=step):
            load_inv[step].wait()
            r = order(step)
            for h in range(2):
                value = dot_nt(bt[pl.ds(h * 256, 256), :], inv_v[r]).reshape(2, 128, 512)
                fp[step, pl.ds(2 * h, 2)] = value
                if step < 3:
                    fsnd[step, pl.ds(2 * h, 2)] = value.astype(BF16)
                for key, (cond, copy) in msgs.items():
                    if key[2] == step and key[3] // 2 == h and key not in later:
                        on(cond, copy.start)

        on(step <= 3 - c, block)
        if step == 0:
            load_pan = pltpu.make_async_copy(pan, big.at[c, pl.ds(0, 3)], ld.at[5])
            load_pan.start()
            load_sinv = pltpu.make_async_copy(sinv, sinv_v, ld.at[6])
            load_sinv.start()
            load_slink = pltpu.make_async_copy(slink, slink_v, ld.at[7])
            load_slink.start()
            load_srhs = pltpu.make_async_copy(
                srhs.at[:, :, pl.ds(pl.multiple_of(c * 128, 128), 128)], srhs_v, ld.at[8]
            )
            load_srhs.start()

    load_pan.wait()
    flows = []

    def flow(sender, number, r, p, to_col):
        copy = remote(big.at[r, p], big.at[r, p], g_ss.at[number], g_rs.at[r, p], leaf, to_col)
        flows.append((c == sender, copy))
        return flows[-1]

    def arrive(r, p):
        remote(big.at[r, p], big.at[r, p], g_ss.at[0], g_rs.at[r, p], leaf, c1).wait_recv()

    def start(*items):
        for cond, copy in items:
            on(cond, copy.start)

    def forward(cond, steps):
        def run():
            for r, p, (_, copy) in steps:
                arrive(r, p)
                copy.start()

        on(cond, run)

    start(*(flow(3, p, 3, p, 0) for p in range(3)), flow(3, 3, 3, 0, 2))
    start(*(flow(2, p, 2, p, 1) for p in range(3)), flow(2, 3, 2, 2, 3))
    start(flow(1, 0, 1, 0, 0), flow(1, 1, 1, 1, 0))
    second = flow(3, 4, 3, 1, 2)

    load_sinv.wait()
    load_slink.wait()
    load_srhs.wait()
    highest = lax.Precision.HIGHEST

    def table(k, carry):
        ik = sinv_v[k]
        kk = jnp.minimum(k, LEVELS - 2)
        gk = lax.dot_general(
            slink_v[kk], ik, (((1,), (0,)), ((), ())), precision=highest, preferred_element_type=F32
        )
        hk = lax.dot_general(ik, ik, (((0,), (0,)), ((), ())), precision=highest, preferred_element_type=F32)
        gh, gl = halves(gk)
        hh, hl = halves(hk)
        wf[k, :, pl.ds(0, 256)] = gh
        wf[k, :, pl.ds(256, 256)] = gh
        wf[k, :, pl.ds(512, 256)] = gl
        for ref, (hi, lo) in ((wi, (hh, hl)), (wg, (gh, gl))):
            ref[k, pl.ds(0, 256), :] = hi
            ref[k, pl.ds(256, 256), :] = hi
            ref[k, pl.ds(512, 256), :] = lo
        rt[k] = srhs_v[k].T
        return carry

    lax.fori_loop(0, LEVELS, table, 0)

    send_meta.wait_recv()
    gap = (
        lax.broadcasted_iota(jnp.int32, (128, 256), 1) - lax.broadcasted_iota(jnp.int32, (128, 256), 0)
    ).astype(F32)
    for k in range(LEVELS):
        for part, ref in enumerate((meta, metarx)):
            spot = jnp.broadcast_to(ref[pl.ds(k, 1), :], (128, 256))
            keep = jnp.broadcast_to(ref[pl.ds(8 + k, 1), :], (128, 256))
            hot = jnp.where(gap == spot, keep, 0.0).astype(BF16)
            est[k, pl.ds(part * 256, 128), :] = hot
            est[k, pl.ds(part * 256 + 128, 128), :] = hot

    def product(r, p):
        return dot_nn(big[r, p], inv_v[r])

    def frecv(slot, from_col):
        remote(frx.at[slot], frx.at[slot], f_ss.at[0], f_rs.at[slot], leaf, from_col).wait_recv()

    def got(slot, from_col):
        frecv(slot, from_col)
        return frx[slot].astype(F32)

    def add_and_send(key, slot, from_col):
        _, _, step, n = key
        fsnd[step, n] = (fp[step, n] + got(slot, from_col)).astype(BF16)
        msgs[key][1].start()

    def solved(r, n, value):
        big[r, 3 + n // 2, pl.ds(n % 2 * 128, 128), :] = value.astype(BF16)

    def after0():
        add_and_send((0, 3, 2, 0), 0, 1)
        add_and_send((0, 3, 2, 1), 1, 1)
        for n in range(4):
            solved(0, n, fp[3, n])

    def after1():
        add_and_send((1, 2, 1, 0), 0, 0)
        add_and_send((1, 2, 1, 1), 1, 0)
        for n in range(4):
            solved(1, n, fp[2, n] + got(2 + n, 0))

    def after2():
        add_and_send((2, 3, 0, 2), 0, 1)
        add_and_send((2, 3, 0, 3), 1, 1)
        for n in (2, 3):
            solved(2, n, fp[1, n] + got(2 + n, 1) + got(4 + n, 3))
        for n in (0, 1):
            solved(2, n, fp[1, n] + got(2 + n, 1))

    def after3():
        for n in range(2):
            frecv(n, 0)
            msgs[3, 2, 9, n][1].start()
        second[1].start()
        for n in (2, 3, 0, 1):
            solved(3, n, fp[0, n] + got(6 + n, 2) + got(2 + n, 0))

    for group, fn in enumerate((after0, after1, after2, after3)):
        on(c == group, fn)

    panels = big[c, pl.ds(0, 3)].reshape(768, 512)

    def share(j):
        rows_j = pl.ds(pl.multiple_of(lax.rem(j, 2) * 128, 128), 128)
        value = dot_nt(big[c, 3 + lax.div(j, 2), rows_j, :], panels).reshape(2, 64, 768)
        cc[j] = value
        cb[j] = value.astype(BF16)

    relay_up = remote(cb.at[c2, 0], prl.at[0], p_ss.at[0], p_rs.at[0], leaf, c1)
    relay_down = remote(cb.at[c2, 1], prl.at[1], p_ss.at[1], p_rs.at[1], leaf, c3)
    direct_up = remote(cb.at[c1, 1], prx.at[q, 0], p_ss.at[2], prx_rs.at[q, 0], base + 1, c1)
    direct_down = remote(cb.at[c3, 0], prx.at[q, 1], p_ss.at[3], prx_rs.at[q, 1], base, c3)
    across = remote(cb.at[c, 1 - q], pon, p_ss.at[4], p_rs.at[2], other, c)
    sum_up = remote(psum.at[0], prx.at[q, 0], p_ss.at[5], prx_rs.at[q, 0], base, c1)
    sum_down = remote(psum.at[1], prx.at[q, 1], p_ss.at[6], prx_rs.at[q, 1], base + 1, c3)
    share(c2)
    relay_up.start()
    relay_down.start()
    share(c1)
    direct_up.start()
    share(c3)
    direct_down.start()
    share(c)
    across.start()
    relay_up.wait_recv()
    psum[0] = (cc[c1, 0] + prl[0].astype(F32)).astype(BF16)
    sum_up.start()
    relay_down.wait_recv()
    psum[1] = (cc[c3, 1] + prl[1].astype(F32)).astype(BF16)
    sum_down.start()
    start(flow(3, 5, 3, 3, 0), flow(3, 6, 3, 4, 0), flow(3, 7, 3, 2, 2), flow(3, 8, 3, 3, 2), flow(3, 9, 3, 4, 2))
    start(flow(2, 4, 2, 3, 1), flow(2, 5, 2, 4, 1), flow(2, 6, 2, 3, 3), flow(2, 7, 2, 4, 3))
    start(flow(1, 2, 1, 2, 0), flow(1, 3, 1, 3, 0), flow(1, 4, 1, 4, 0))
    forward(c == 3, [(2, 2, flow(3, 10, 2, 2, 0))])
    forward(c == 2, [(3, 0, flow(2, 8, 3, 0, 1)), (3, 1, flow(2, 9, 3, 1, 1))])
    forward(c == 1, [(2, 0, flow(1, 5, 2, 0, 0)), (2, 1, flow(1, 6, 2, 1, 0))])
    forward(c == 0, [(3, 2, flow(0, 0, 3, 2, 1))])
    across.wait_recv()

    def precv(p, d, from_col):
        remote(prx.at[p, d], prx.at[p, d], p_ss.at[0], prx_rs.at[p, d], base + p, from_col).wait_recv()

    for p in range(2):
        precv(p, 0, c3)
        precv(p, 1, c1)
    mine = cc[c, q] + prx[q, 0].astype(F32) + prx[q, 1].astype(F32)
    theirs = pon[...].astype(F32) + prx[1 - q, 0].astype(F32) + prx[1 - q, 1].astype(F32)
    mh, ml = halves(mine)
    th, tl = halves(theirs)
    for k in range(LEVELS):
        at = slice(k * 128, k * 128 + 128)
        left = jnp.concatenate([mh[:, at], ml[:, at], th[:, at], tl[:, at]], axis=1)
        u[k] = dot_nn(left, est[k])

    mine_rows = pl.ds(pl.multiple_of(q * 64, 64), 64)

    def tree(k, j):
        n = PAIRS.index((k, j))
        return remote(tsnd.at[n], trx.at[n], t_ss.at[n], t_rs.at[n], leaf ^ MASKS[k], c)

    def send(k, j):
        tsnd[PAIRS.index((k, j))] = u[j].astype(HOP)
        tree(k, j).start()

    def receive(k, j):
        tree(k, j).wait_recv()
        u[j] = u[j] + trx[PAIRS.index((k, j))].astype(F32)

    for k in range(LEVELS):
        if k > 0:
            receive(k, k)
        right = wide(rt[k, mine_rows, :] - u[k])
        if k + 1 < LEVELS:
            linked = dot_nt(right, wf[k])
            if k > 0:
                receive(k, k + 1)
            u[k + 1] = u[k + 1] + linked
            send(k + 1, k + 1)
            for j in range(k + 2, LEVELS):
                if k > 0:
                    receive(k, j)
                send(k + 1, j)
        fs[k] = dot_nn(right, wi[k])
        if k < 5:
            acc[k] = product(c, k)
        if k == 3:
            forward(c == 3, [(2, 3, flow(3, 11, 2, 3, 0)), (2, 4, flow(3, 12, 2, 4, 0))])
            forward(c == 2, [(3, 3, flow(2, 10, 3, 3, 1))])
            forward(c == 0, [(3, 4, flow(0, 1, 3, 4, 1))])
    slot = c * 2 + q
    near, far = jnp.where(q == 0, c3, c1), jnp.where(q == 0, c1, c3)
    swap = remote(ball.at[:, mine_rows, :], ball.at[:, mine_rows, :], b_ss, b_rs, other, c)
    s_copies = []

    def block_of(ref, g):
        return ref.at[:, pl.ds(256 * g, 256)]

    for g in (2, 1, 0):
        for k in (2 * g + 1, 2 * g):
            down = fs[k]
            if k + 1 < LEVELS:
                down = down - dot_nn(wide(bs[k + 1]), wg[k])
            bs[k] = down
            ball[k, mine_rows, :] = down
            low = down.astype(BF16)
            at = slice(k * 128, k * 128 + 128)
            sall[slot, :, at] = dot_nt(low, est[k, pl.ds(0, 128), :]).astype(BF16)
            soth[:, at] = dot_nt(low, est[k, pl.ds(256, 128), :]).astype(BF16)
        mine_g, to_g = block_of(sall.at[slot], g), block_of(sall.at[slot], g)
        for n, (src, to_leaf, to_col) in enumerate(
            ((mine_g, leaf, c1), (mine_g, leaf, c3), (block_of(soth, g), other, c1),
             (block_of(soth, g), other, c3), (block_of(soth, g), other, c))
        ):
            s_copies.append(remote(src, to_g, s_ss.at[n, g], s_rs.at[slot, g], to_leaf, to_col))
            s_copies[-1].start()
    swap.start()

    def srecv(at, g, from_leaf, from_col):
        ref = block_of(sall.at[at], g)
        remote(ref, ref, s_ss.at[0, g], s_rs.at[at, g], from_leaf, from_col).wait_recv()

    relays = []
    for g in (2, 1, 0):
        for p in range(2):
            at = near * 2 + p
            srecv(at, g, base + p, near)
            ref = block_of(sall.at[at], g)
            relays.append(remote(ref, ref, s_ss.at[5 + p, g], s_rs.at[at, g], leaf, far))
            relays[-1].start()

    remote(ball.at[:, mine_rows, :], ball.at[:, mine_rows, :], b_ss, b_rs, other, c).wait_send()
    theirs_rows = pl.ds(pl.multiple_of((1 - q) * 64, 64), 64)
    remote(ball.at[:, theirs_rows, :], ball.at[:, theirs_rows, :], b_ss, b_rs, other, c).wait_recv()
    for k in range(LEVELS):
        solt[k] = ball[k].T
    put_sol = pltpu.make_async_copy(solt, sol_out, o_s.at[0])
    put_sol.start()

    for step in range(1, 4):

        def add(step=step):
            r = c + step
            for p in range(5):
                taken = (c == 0) & (r == 3) & (p in (2, 4))
                taken |= (c == 1) & (r == 2) & (p in (0, 1))
                taken |= (c == 2) & (r == 3) & (p in (0, 1, 3))
                on(jnp.logical_not(taken), functools.partial(arrive, r, p))
                acc[p] += product(r, p)

        on(c + step <= 3, add)

    weights = acc[pl.ds(0, 3)].reshape(768, 512).astype(BF16)
    puts = []

    def final(y):
        taken = sall[pl.ds(2 * y, 2)].reshape(128, 768)
        rows_y = pl.ds(pl.multiple_of(lax.rem(y, 2) * 128, 128), 128)
        to = pl.ds(pl.multiple_of(y * 128, 128), 128)
        value = acc[3 + lax.div(y, 2), rows_y, :] - dot_nn(taken, weights)
        xt[:, to] = value.T.astype(BF16)
        puts.append(pltpu.make_async_copy(xt.at[:, to], x_out.at[:, to], o_s.at[1 + len(puts)]))
        puts[-1].start()

    for g in range(3):
        srecv(c * 2 + 1 - q, g, other, c)
    final(c)
    final(near)
    for p in range(2):
        for g in range(3):
            srecv(far * 2 + p, g, base + p, far)
    final(far)
    for p in range(2):
        for g in range(3):
            srecv(c2 * 2 + p, g, leaf, near)
    final(c2)

    for copy in (send_meta, relay_up, relay_down, direct_up, direct_down, across, sum_up, sum_down, *s_copies, *relays):
        copy.wait_send()
    for k, j in PAIRS:
        tree(k, j).wait_send()
    for cond, copy in (*msgs.values(), *flows):
        on(cond, copy.wait_send)
    put_sol.wait()
    for put in puts:
        put.wait()


def write_out(x, sol, x_out, sol_out, sems):
    copies = [pltpu.make_async_copy(x, x_out, sems.at[0]), pltpu.make_async_copy(sol, sol_out, sems.at[1])]
    for copy in copies:
        copy.start()
    for copy in copies:
        copy.wait()


def on_device(leaf_rhs, leaf_inverse, panels, pattern, offsets, sep_inverse, sep_link, sep_rhs):
    anywhere = pl.BlockSpec(memory_space=pl.ANY)
    in_hbm = functools.partial(pltpu.with_memory_space_constraint, memory_space=pltpu.HBM)
    hbm = pl.BlockSpec(memory_space=pltpu.HBM)
    scalars = pl.BlockSpec(memory_space=pltpu.SMEM)
    dma = pltpu.SemaphoreType.DMA
    messages = len(PAIRS)
    x, sol = pl.pallas_call(
        kernel,
        out_shape=(jax.ShapeDtypeStruct((512, 512), BF16), jax.ShapeDtypeStruct((6, 256, 128), F32)),
        in_specs=[hbm, hbm, hbm, scalars, scalars, hbm, hbm, hbm],
        out_specs=(anywhere, anywhere),
        scratch_shapes=[
            pltpu.VMEM((512, 512), BF16),
            pltpu.VMEM((4, 512, 512), BF16),
            pltpu.VMEM((4, 5, 256, 512), BF16),
            pltpu.VMEM((6, 256, 256), F32),
            pltpu.VMEM((5, 256, 256), F32),
            pltpu.VMEM((6, 256, 128), F32),
            pltpu.VMEM((512, 512), BF16),
            pltpu.VMEM((4, 4, 128, 512), F32),
            pltpu.VMEM((3, 4, 128, 512), BF16),
            pltpu.VMEM((10, 128, 512), BF16),
            pltpu.VMEM((4, 2, 64, 768), F32),
            pltpu.VMEM((4, 2, 64, 768), BF16),
            pltpu.VMEM((2, 64, 768), BF16),
            pltpu.VMEM((2, 64, 768), BF16),
            pltpu.VMEM((2, 2, 64, 768), BF16),
            pltpu.VMEM((64, 768), BF16),
            pltpu.VMEM((16, 256), F32),
            pltpu.VMEM((16, 256), F32),
            pltpu.VMEM((6, 512, 256), BF16),
            pltpu.VMEM((6, 256, 768), BF16),
            pltpu.VMEM((6, 768, 256), BF16),
            pltpu.VMEM((6, 768, 256), BF16),
            pltpu.VMEM((6, 128, 256), F32),
            pltpu.VMEM((6, 64, 256), F32),
            pltpu.VMEM((6, 64, 256), F32),
            pltpu.VMEM((6, 64, 256), F32),
            pltpu.VMEM((messages, 64, 256), HOP),
            pltpu.VMEM((messages, 64, 256), HOP),
            pltpu.VMEM((6, 128, 256), F32),
            pltpu.VMEM((6, 256, 128), F32),
            pltpu.VMEM((64, 768), BF16),
            pltpu.VMEM((8, 64, 768), BF16),
            pltpu.VMEM((5, 256, 512), F32),
            pltpu.VMEM((512, 512), BF16),
            dma((9,)),
            dma((12,)),
            dma((10,)),
            dma((7,)),
            dma((3,)),
            dma((2, 2)),
            dma,
            dma,
            dma((messages,)),
            dma((messages,)),
            dma,
            dma,
            dma((7, 3)),
            dma((8, 3)),
            dma((13,)),
            dma((4, 5)),
            dma((5,)),
        ],
        compiler_params=pltpu.CompilerParams(
            collective_id=0, has_side_effects=True, vmem_limit_bytes=46 * 1024 * 1024
        ),
    )(
        in_hbm(leaf_rhs[0]),
        in_hbm(leaf_inverse[0]),
        in_hbm(panels[0].reshape(3, 256, 512)),
        in_hbm(pattern),
        in_hbm(offsets),
        in_hbm(sep_inverse[0]),
        in_hbm(sep_link[0]),
        in_hbm(sep_rhs[0]),
    )
    x, sol = pl.pallas_call(
        write_out,
        out_shape=(jax.ShapeDtypeStruct((512, 512), BF16), jax.ShapeDtypeStruct((6, 256, 128), F32)),
        in_specs=[anywhere, anywhere],
        out_specs=(anywhere, anywhere),
        scratch_shapes=[dma((2,))],
        compiler_params=pltpu.CompilerParams(vmem_limit_bytes=1024 * 1024),
    )(x, sol)
    return x[None], sol[None]


def solution(mesh):
    in_specs = (
        P("leaf", "col", None),
        P("leaf", None, "col"),
        P("leaf", None, None, "col"),
        P("leaf", None),
        P("leaf", None),
        P("leaf", None, None, None),
        P("leaf", None, None, None),
        P("leaf", None, None, None),
    )
    out_specs = (P("leaf", "col", None), P("leaf", None, None, "col"))
    return jax.shard_map(on_device, mesh=mesh, in_specs=in_specs, out_specs=out_specs, check_vma=False)
```

```python
import functools

import jax
import jax.numpy as jnp
from jax import lax
from jax.experimental import pallas as pl
from jax.experimental.pallas import tpu as pltpu
from jax.sharding import PartitionSpec as P

MESH = pl.DeviceIdType.MESH
F32 = jnp.float32
BF16 = jnp.bfloat16
HOP = BF16
LEVELS = 6
MASKS = (1, 2, 6, 8, 16, 56)
PASSED = {0: {(3, 2), (3, 4)}, 1: {(2, 0), (2, 1)}, 2: {(3, 0), (3, 1), (3, 3)}}
EARLY = {
    0: {0: ((3, 0), (1, 0)), 1: ((3, 1), (1, 1)), 2: ((3, 2), (1, 2)), 3: ((3, 3),), 4: ((3, 4), (1, 3), (1, 4))},
    1: {0: ((2, 0),), 1: ((2, 1),), 2: ((2, 2),), 4: ((2, 3), (2, 4))},
    2: {4: ((3, 0), (3, 1))},
}
PAIRS = tuple((k, j) for k in range(1, LEVELS) for j in range(k, LEVELS))


def dot_nn(a, b):
    return lax.dot_general(a, b, (((1,), (0,)), ((), ())), preferred_element_type=F32)


def dot_nt(a, b):
    return lax.dot_general(a, b, (((1,), (1,)), ((), ())), preferred_element_type=F32)


def halves(value):
    high = value.astype(BF16)
    return high, (value - high.astype(F32)).astype(BF16)


def wide(value):
    high, low = halves(value)
    return jnp.concatenate([high, low, high], axis=1)


def kernel(
    rhs, inv, pan, pat, off, sinv, slink, srhs, x_out, sol_out,
    rhs_v, inv_v, big, sinv_v, slink_v, srhs_v,
    bt, fp, fsnd, frx, cc, cb, prl, psum, prx, pon, meta, metarx, est,
    wf, wi, wg, rt, u, fs, bs, tsnd, trx, ball, solt, soth, sall, acc, xt,
    ld, f_ss, f_rs, p_ss, p_rs, prx_rs, m_ss, m_rs, t_ss, t_rs, b_ss, b_rs, s_ss, s_rs, g_ss, g_rs, o_s,
):
    leaf = lax.axis_index("leaf")
    c = lax.axis_index("col")
    q = lax.rem(leaf, 2)
    base = leaf - q
    c1, c2, c3 = lax.rem(c + 1, 4), lax.rem(c + 2, 4), lax.rem(c + 3, 4)
    rows = 512

    def remote(src, dst, ss, rs, to_leaf, to_col):
        return pltpu.make_async_remote_copy(
            src_ref=src, dst_ref=dst, send_sem=ss, recv_sem=rs,
            device_id=(to_leaf, to_col), device_id_type=MESH,
        )

    sent = []

    def on(cond, fn):
        pl.when(cond)(fn)

    def order(step):
        return jnp.where(c == 0, (2, 1, 3, 0)[step], 3 - step)

    load_rhs = pltpu.make_async_copy(rhs, rhs_v, ld.at[0])
    load_rhs.start()
    load_inv = []
    for step in range(4):
        r = jnp.maximum(order(step), 0)
        load_inv.append(
            pltpu.make_async_copy(inv.at[pl.ds(pl.multiple_of(r * rows, rows), rows)], inv_v.at[r], ld.at[1 + step])
        )
        on(step <= 3 - c, load_inv[step].start)
    peers = [(leaf, c1), (leaf, c2), (leaf, c3)]
    peers += [(base + 1 - q, cc_) for cc_ in (c, c1, c2, c3)]
    peers += [(leaf ^ MASKS[k], c) for k in range(1, LEVELS)]
    barrier = pltpu.get_barrier_semaphore()
    for peer in peers:
        pl.semaphore_signal(barrier, inc=1, device_id=peer, device_id_type=MESH)

    for k in range(LEVELS):
        meta[pl.ds(k, 1), :] = jnp.full((1, 256), off[0, k].astype(F32), F32)
        meta[pl.ds(8 + k, 1), :] = jnp.full((1, 256), pat[0, k].astype(F32), F32)

    load_rhs.wait()
    bt[...] = rhs_v[...].T
    pl.semaphore_wait(barrier, len(peers))

    other = base + 1 - q
    send_meta = remote(meta, metarx, m_ss, m_rs, other, c)
    send_meta.start()

    def fmsg(sender, number, src, slot, to_col):
        return (c == sender, remote(src, frx.at[slot], f_ss.at[number], f_rs.at[slot], leaf, to_col))

    msgs = {}

    def messages(sender, to_col, items):
        for step, n, slot in items:
            number = sum(1 for key in msgs if key[0] == sender)
            msgs[sender, to_col, step, n] = fmsg(sender, number, fsnd.at[step, n], slot, to_col)

    messages(0, 1, [(0, 0, 0), (0, 1, 1), (1, 0, 2), (1, 1, 3), (1, 2, 4), (1, 3, 5)])
    messages(0, 3, [(0, 2, 0), (0, 3, 1), (2, 2, 4), (2, 3, 5), (2, 0, 2), (2, 1, 3)])
    messages(1, 0, [(0, 0, 0), (0, 1, 1)])
    messages(1, 2, [(0, 2, 0), (0, 3, 1), (1, 2, 4), (1, 3, 5), (1, 0, 2), (1, 1, 3)])
    messages(2, 3, [(0, 0, 6), (0, 1, 7), (0, 2, 8), (0, 3, 9)])
    msgs[3, 2, 9, 0] = fmsg(3, 0, frx.at[0], 6, 2)
    msgs[3, 2, 9, 1] = fmsg(3, 1, frx.at[1], 7, 2)
    later = {(0, 3, 2, 0), (0, 3, 2, 1), (1, 2, 1, 0), (1, 2, 1, 1), (2, 3, 0, 2), (2, 3, 0, 3)}
    for step in range(4):

        def block(step=step):
            load_inv[step].wait()
            r = order(step)
            for h in range(2):
                value = dot_nt(bt[pl.ds(h * 256, 256), :], inv_v[r]).reshape(2, 128, 512)
                fp[step, pl.ds(2 * h, 2)] = value
                if step < 3:
                    fsnd[step, pl.ds(2 * h, 2)] = value.astype(BF16)
                for key, (cond, copy) in msgs.items():
                    if key[2] == step and key[3] // 2 == h and key not in later:
                        on(cond, copy.start)

        on(step <= 3 - c, block)
        if step == 0:
            load_pan = pltpu.make_async_copy(pan, big.at[c, pl.ds(0, 3)], ld.at[5])
            load_pan.start()
            load_sinv = pltpu.make_async_copy(sinv, sinv_v, ld.at[6])
            load_sinv.start()
            load_slink = pltpu.make_async_copy(slink, slink_v, ld.at[7])
            load_slink.start()
            load_srhs = pltpu.make_async_copy(
                srhs.at[:, :, pl.ds(pl.multiple_of(c * 128, 128), 128)], srhs_v, ld.at[8]
            )
            load_srhs.start()

    load_pan.wait()
    flows = []

    def flow(sender, number, r, p, to_col):
        copy = remote(big.at[r, p], big.at[r, p], g_ss.at[number], g_rs.at[r, p], leaf, to_col)
        flows.append((c == sender, copy))
        return flows[-1]

    def arrive(r, p):
        remote(big.at[r, p], big.at[r, p], g_ss.at[0], g_rs.at[r, p], leaf, c1).wait_recv()

    def start(*items):
        for cond, copy in items:
            on(cond, copy.start)

    def forward(cond, steps):
        def run():
            for r, p, (_, copy) in steps:
                arrive(r, p)
                copy.start()

        on(cond, run)

    start(*(flow(3, p, 3, p, 0) for p in range(3)), flow(3, 3, 3, 0, 2))
    start(*(flow(2, p, 2, p, 1) for p in range(3)), flow(2, 3, 2, 2, 3))
    start(flow(1, 0, 1, 0, 0), flow(1, 1, 1, 1, 0))
    second = flow(3, 4, 3, 1, 2)

    load_sinv.wait()
    load_slink.wait()
    load_srhs.wait()
    highest = lax.Precision.HIGHEST

    def table(k, carry):
        ik = sinv_v[k]
        kk = jnp.minimum(k, LEVELS - 2)
        gk = lax.dot_general(
            slink_v[kk], ik, (((1,), (0,)), ((), ())), precision=highest, preferred_element_type=F32
        )
        hk = lax.dot_general(ik, ik, (((0,), (0,)), ((), ())), precision=highest, preferred_element_type=F32)
        gh, gl = halves(gk)
        hh, hl = halves(hk)
        wf[k, :, pl.ds(0, 256)] = gh
        wf[k, :, pl.ds(256, 256)] = gh
        wf[k, :, pl.ds(512, 256)] = gl
        for ref, (hi, lo) in ((wi, (hh, hl)), (wg, (gh, gl))):
            ref[k, pl.ds(0, 256), :] = hi
            ref[k, pl.ds(256, 256), :] = hi
            ref[k, pl.ds(512, 256), :] = lo
        rt[k] = srhs_v[k].T
        return carry

    lax.fori_loop(0, LEVELS, table, 0)

    send_meta.wait_recv()
    gap = (
        lax.broadcasted_iota(jnp.int32, (128, 256), 1) - lax.broadcasted_iota(jnp.int32, (128, 256), 0)
    ).astype(F32)
    for k in range(LEVELS):
        for part, ref in enumerate((meta, metarx)):
            spot = jnp.broadcast_to(ref[pl.ds(k, 1), :], (128, 256))
            keep = jnp.broadcast_to(ref[pl.ds(8 + k, 1), :], (128, 256))
            hot = jnp.where(gap == spot, keep, 0.0).astype(BF16)
            est[k, pl.ds(part * 256, 128), :] = hot
            est[k, pl.ds(part * 256 + 128, 128), :] = hot

    def product(r, p):
        return dot_nn(big[r, p], inv_v[r])

    def frecv(slot, from_col):
        remote(frx.at[slot], frx.at[slot], f_ss.at[0], f_rs.at[slot], leaf, from_col).wait_recv()

    def got(slot, from_col):
        frecv(slot, from_col)
        return frx[slot].astype(F32)

    def add_and_send(key, slot, from_col):
        _, _, step, n = key
        fsnd[step, n] = (fp[step, n] + got(slot, from_col)).astype(BF16)
        msgs[key][1].start()

    def solved(r, n, value):
        big[r, 3 + n // 2, pl.ds(n % 2 * 128, 128), :] = value.astype(BF16)

    def after0():
        add_and_send((0, 3, 2, 0), 0, 1)
        add_and_send((0, 3, 2, 1), 1, 1)
        for n in range(4):
            solved(0, n, fp[3, n])

    def after1():
        add_and_send((1, 2, 1, 0), 0, 0)
        add_and_send((1, 2, 1, 1), 1, 0)
        for n in range(4):
            solved(1, n, fp[2, n] + got(2 + n, 0))

    def after2():
        add_and_send((2, 3, 0, 2), 0, 1)
        add_and_send((2, 3, 0, 3), 1, 1)
        for n in (2, 3):
            solved(2, n, fp[1, n] + got(2 + n, 1) + got(4 + n, 3))
        for n in (0, 1):
            solved(2, n, fp[1, n] + got(2 + n, 1))

    def after3():
        for n in range(2):
            frecv(n, 0)
            msgs[3, 2, 9, n][1].start()
        second[1].start()
        for n in (2, 3, 0, 1):
            solved(3, n, fp[0, n] + got(6 + n, 2) + got(2 + n, 0))

    for group, fn in enumerate((after0, after1, after2, after3)):
        on(c == group, fn)

    panels = big[c, pl.ds(0, 3)].reshape(768, 512)

    def share(j):
        rows_j = pl.ds(pl.multiple_of(lax.rem(j, 2) * 128, 128), 128)
        value = dot_nt(big[c, 3 + lax.div(j, 2), rows_j, :], panels).reshape(2, 64, 768)
        cc[j] = value
        cb[j] = value.astype(BF16)

    relay_up = remote(cb.at[c2, 0], prl.at[0], p_ss.at[0], p_rs.at[0], leaf, c1)
    relay_down = remote(cb.at[c2, 1], prl.at[1], p_ss.at[1], p_rs.at[1], leaf, c3)
    direct_up = remote(cb.at[c1, 1], prx.at[q, 0], p_ss.at[2], prx_rs.at[q, 0], base + 1, c1)
    direct_down = remote(cb.at[c3, 0], prx.at[q, 1], p_ss.at[3], prx_rs.at[q, 1], base, c3)
    across = remote(cb.at[c, 1 - q], pon, p_ss.at[4], p_rs.at[2], other, c)
    sum_up = remote(psum.at[0], prx.at[q, 0], p_ss.at[5], prx_rs.at[q, 0], base, c1)
    sum_down = remote(psum.at[1], prx.at[q, 1], p_ss.at[6], prx_rs.at[q, 1], base + 1, c3)
    share(c2)
    relay_up.start()
    relay_down.start()
    share(c1)
    direct_up.start()
    share(c3)
    direct_down.start()
    share(c)
    across.start()
    relay_up.wait_recv()
    psum[0] = (cc[c1, 0] + prl[0].astype(F32)).astype(BF16)
    sum_up.start()
    relay_down.wait_recv()
    psum[1] = (cc[c3, 1] + prl[1].astype(F32)).astype(BF16)
    sum_down.start()
    start(flow(3, 5, 3, 3, 0), flow(3, 6, 3, 4, 0), flow(3, 7, 3, 2, 2), flow(3, 8, 3, 3, 2), flow(3, 9, 3, 4, 2))
    start(flow(2, 4, 2, 3, 1), flow(2, 5, 2, 4, 1), flow(2, 6, 2, 3, 3), flow(2, 7, 2, 4, 3))
    start(flow(1, 2, 1, 2, 0), flow(1, 3, 1, 3, 0), flow(1, 4, 1, 4, 0))
    forward(c == 3, [(2, 2, flow(3, 10, 2, 2, 0))])
    forward(c == 2, [(3, 0, flow(2, 8, 3, 0, 1)), (3, 1, flow(2, 9, 3, 1, 1))])
    forward(c == 1, [(2, 0, flow(1, 5, 2, 0, 0)), (2, 1, flow(1, 6, 2, 1, 0))])
    forward(c == 0, [(3, 2, flow(0, 0, 3, 2, 1))])
    across.wait_recv()

    def precv(p, d, from_col):
        remote(prx.at[p, d], prx.at[p, d], p_ss.at[0], prx_rs.at[p, d], base + p, from_col).wait_recv()

    for p in range(2):
        precv(p, 0, c3)
        precv(p, 1, c1)
    mine = cc[c, q] + prx[q, 0].astype(F32) + prx[q, 1].astype(F32)
    theirs = pon[...].astype(F32) + prx[1 - q, 0].astype(F32) + prx[1 - q, 1].astype(F32)
    mh, ml = halves(mine)
    th, tl = halves(theirs)
    for k in range(LEVELS):
        at = slice(k * 128, k * 128 + 128)
        left = jnp.concatenate([mh[:, at], ml[:, at], th[:, at], tl[:, at]], axis=1)
        u[k] = dot_nn(left, est[k])

    mine_rows = pl.ds(pl.multiple_of(q * 64, 64), 64)

    def tree(k, j):
        n = PAIRS.index((k, j))
        return remote(tsnd.at[n], trx.at[n], t_ss.at[n], t_rs.at[n], leaf ^ MASKS[k], c)

    def send(k, j):
        tsnd[PAIRS.index((k, j))] = u[j].astype(HOP)
        tree(k, j).start()

    def receive(k, j):
        tree(k, j).wait_recv()
        u[j] = u[j] + trx[PAIRS.index((k, j))].astype(F32)

    for k in range(LEVELS):
        if k > 0:
            receive(k, k)
        right = wide(rt[k, mine_rows, :] - u[k])
        if k + 1 < LEVELS:
            linked = dot_nt(right, wf[k])
            if k > 0:
                receive(k, k + 1)
            u[k + 1] = u[k + 1] + linked
            send(k + 1, k + 1)
            for j in range(k + 2, LEVELS):
                if k > 0:
                    receive(k, j)
                send(k + 1, j)
        fs[k] = dot_nn(right, wi[k])
        if k < 5:
            acc[k] = product(c, k)
        if k == 3:
            forward(c == 3, [(2, 3, flow(3, 11, 2, 3, 0)), (2, 4, flow(3, 12, 2, 4, 0))])
            forward(c == 2, [(3, 3, flow(2, 10, 3, 3, 1))])
            forward(c == 0, [(3, 4, flow(0, 1, 3, 4, 1))])
        for group, windows in EARLY.items():
            if k in windows:

                def early(group=group, pieces=windows[k]):
                    for r, p in pieces:
                        if (r, p) not in PASSED[group]:
                            arrive(r, p)
                        acc[p] += product(r, p)

                on(c == group, early)
    slot = c * 2 + q
    near, far = jnp.where(q == 0, c3, c1), jnp.where(q == 0, c1, c3)
    swap = remote(ball.at[:, mine_rows, :], ball.at[:, mine_rows, :], b_ss, b_rs, other, c)
    s_copies = []

    def block_of(ref, g):
        return ref.at[:, pl.ds(256 * g, 256)]

    for g in (2, 1, 0):
        for k in (2 * g + 1, 2 * g):
            down = fs[k]
            if k + 1 < LEVELS:
                down = down - dot_nn(wide(bs[k + 1]), wg[k])
            bs[k] = down
            ball[k, mine_rows, :] = down
            low = down.astype(BF16)
            at = slice(k * 128, k * 128 + 128)
            sall[slot, :, at] = dot_nt(low, est[k, pl.ds(0, 128), :]).astype(BF16)
            soth[:, at] = dot_nt(low, est[k, pl.ds(256, 128), :]).astype(BF16)
        mine_g, to_g = block_of(sall.at[slot], g), block_of(sall.at[slot], g)
        for n, (src, to_leaf, to_col) in enumerate(
            ((mine_g, leaf, c1), (mine_g, leaf, c3), (block_of(soth, g), other, c1),
             (block_of(soth, g), other, c3), (block_of(soth, g), other, c))
        ):
            s_copies.append(remote(src, to_g, s_ss.at[n, g], s_rs.at[slot, g], to_leaf, to_col))
            s_copies[-1].start()
    swap.start()

    def srecv(at, g, from_leaf, from_col):
        ref = block_of(sall.at[at], g)
        remote(ref, ref, s_ss.at[0, g], s_rs.at[at, g], from_leaf, from_col).wait_recv()

    relays = []
    for g in (2, 1, 0):
        for p in range(2):
            at = near * 2 + p
            srecv(at, g, base + p, near)
            ref = block_of(sall.at[at], g)
            relays.append(remote(ref, ref, s_ss.at[5 + p, g], s_rs.at[at, g], leaf, far))
            relays[-1].start()

    remote(ball.at[:, mine_rows, :], ball.at[:, mine_rows, :], b_ss, b_rs, other, c).wait_send()
    theirs_rows = pl.ds(pl.multiple_of((1 - q) * 64, 64), 64)
    remote(ball.at[:, theirs_rows, :], ball.at[:, theirs_rows, :], b_ss, b_rs, other, c).wait_recv()
    for k in range(LEVELS):
        solt[k] = ball[k].T
    put_sol = pltpu.make_async_copy(solt, sol_out, o_s.at[0])
    put_sol.start()

    for group in range(3):

        def rest(group=group):
            done = {piece for pieces in EARLY.get(group, {}).values() for piece in pieces}
            for r in range(group + 1, 4):
                for p in range(5):
                    if (r, p) not in done:
                        if (r, p) not in PASSED[group]:
                            arrive(r, p)
                        acc[p] += product(r, p)

        on(c == group, rest)

    weights = acc[pl.ds(0, 3)].reshape(768, 512).astype(BF16)
    puts = []

    def final(y):
        taken = sall[pl.ds(2 * y, 2)].reshape(128, 768)
        rows_y = pl.ds(pl.multiple_of(lax.rem(y, 2) * 128, 128), 128)
        to = pl.ds(pl.multiple_of(y * 128, 128), 128)
        value = acc[3 + lax.div(y, 2), rows_y, :] - dot_nn(taken, weights)
        xt[:, to] = value.T.astype(BF16)
        puts.append(pltpu.make_async_copy(xt.at[:, to], x_out.at[:, to], o_s.at[1 + len(puts)]))
        puts[-1].start()

    for g in range(3):
        srecv(c * 2 + 1 - q, g, other, c)
    final(c)
    final(near)
    for p in range(2):
        for g in range(3):
            srecv(far * 2 + p, g, base + p, far)
    final(far)
    for p in range(2):
        for g in range(3):
            srecv(c2 * 2 + p, g, leaf, near)
    final(c2)

    for copy in (send_meta, relay_up, relay_down, direct_up, direct_down, across, sum_up, sum_down, *s_copies, *relays):
        copy.wait_send()
    for k, j in PAIRS:
        tree(k, j).wait_send()
    for cond, copy in (*msgs.values(), *flows):
        on(cond, copy.wait_send)
    put_sol.wait()
    for put in puts:
        put.wait()


def write_out(x, sol, x_out, sol_out, sems):
    copies = [pltpu.make_async_copy(x, x_out, sems.at[0]), pltpu.make_async_copy(sol, sol_out, sems.at[1])]
    for copy in copies:
        copy.start()
    for copy in copies:
        copy.wait()


def on_device(leaf_rhs, leaf_inverse, panels, pattern, offsets, sep_inverse, sep_link, sep_rhs):
    anywhere = pl.BlockSpec(memory_space=pl.ANY)
    in_hbm = functools.partial(pltpu.with_memory_space_constraint, memory_space=pltpu.HBM)
    hbm = pl.BlockSpec(memory_space=pltpu.HBM)
    scalars = pl.BlockSpec(memory_space=pltpu.SMEM)
    dma = pltpu.SemaphoreType.DMA
    messages = len(PAIRS)
    x, sol = pl.pallas_call(
        kernel,
        out_shape=(jax.ShapeDtypeStruct((512, 512), BF16), jax.ShapeDtypeStruct((6, 256, 128), F32)),
        in_specs=[hbm, hbm, hbm, scalars, scalars, hbm, hbm, hbm],
        out_specs=(anywhere, anywhere),
        scratch_shapes=[
            pltpu.VMEM((512, 512), BF16),
            pltpu.VMEM((4, 512, 512), BF16),
            pltpu.VMEM((4, 5, 256, 512), BF16),
            pltpu.VMEM((6, 256, 256), F32),
            pltpu.VMEM((5, 256, 256), F32),
            pltpu.VMEM((6, 256, 128), F32),
            pltpu.VMEM((512, 512), BF16),
            pltpu.VMEM((4, 4, 128, 512), F32),
            pltpu.VMEM((3, 4, 128, 512), BF16),
            pltpu.VMEM((10, 128, 512), BF16),
            pltpu.VMEM((4, 2, 64, 768), F32),
            pltpu.VMEM((4, 2, 64, 768), BF16),
            pltpu.VMEM((2, 64, 768), BF16),
            pltpu.VMEM((2, 64, 768), BF16),
            pltpu.VMEM((2, 2, 64, 768), BF16),
            pltpu.VMEM((64, 768), BF16),
            pltpu.VMEM((16, 256), F32),
            pltpu.VMEM((16, 256), F32),
            pltpu.VMEM((6, 512, 256), BF16),
            pltpu.VMEM((6, 256, 768), BF16),
            pltpu.VMEM((6, 768, 256), BF16),
            pltpu.VMEM((6, 768, 256), BF16),
            pltpu.VMEM((6, 128, 256), F32),
            pltpu.VMEM((6, 64, 256), F32),
            pltpu.VMEM((6, 64, 256), F32),
            pltpu.VMEM((6, 64, 256), F32),
            pltpu.VMEM((messages, 64, 256), HOP),
            pltpu.VMEM((messages, 64, 256), HOP),
            pltpu.VMEM((6, 128, 256), F32),
            pltpu.VMEM((6, 256, 128), F32),
            pltpu.VMEM((64, 768), BF16),
            pltpu.VMEM((8, 64, 768), BF16),
            pltpu.VMEM((5, 256, 512), F32),
            pltpu.VMEM((512, 512), BF16),
            dma((9,)),
            dma((12,)),
            dma((10,)),
            dma((7,)),
            dma((3,)),
            dma((2, 2)),
            dma,
            dma,
            dma((messages,)),
            dma((messages,)),
            dma,
            dma,
            dma((7, 3)),
            dma((8, 3)),
            dma((13,)),
            dma((4, 5)),
            dma((5,)),
        ],
        compiler_params=pltpu.CompilerParams(
            collective_id=0, has_side_effects=True, vmem_limit_bytes=46 * 1024 * 1024
        ),
    )(
        in_hbm(leaf_rhs[0]),
        in_hbm(leaf_inverse[0]),
        in_hbm(panels[0].reshape(3, 256, 512)),
        in_hbm(pattern),
        in_hbm(offsets),
        in_hbm(sep_inverse[0]),
        in_hbm(sep_link[0]),
        in_hbm(sep_rhs[0]),
    )
    x, sol = pl.pallas_call(
        write_out,
        out_shape=(jax.ShapeDtypeStruct((512, 512), BF16), jax.ShapeDtypeStruct((6, 256, 128), F32)),
        in_specs=[anywhere, anywhere],
        out_specs=(anywhere, anywhere),
        scratch_shapes=[dma((2,))],
        compiler_params=pltpu.CompilerParams(vmem_limit_bytes=1024 * 1024),
    )(x, sol)
    return x[None], sol[None]


def solution(mesh):
    in_specs = (
        P("leaf", "col", None),
        P("leaf", None, "col"),
        P("leaf", None, None, "col"),
        P("leaf", None),
        P("leaf", None),
        P("leaf", None, None, None),
        P("leaf", None, None, None),
        P("leaf", None, None, None),
    )
    out_specs = (P("leaf", "col", None), P("leaf", None, None, "col"))
    return jax.shard_map(on_device, mesh=mesh, in_specs=in_specs, out_specs=out_specs, check_vma=False)
```

```python
import functools

import jax
import jax.numpy as jnp
from jax import lax
from jax.experimental import pallas as pl
from jax.experimental.pallas import tpu as pltpu
from jax.sharding import PartitionSpec as P

MESH = pl.DeviceIdType.MESH
F32 = jnp.float32
BF16 = jnp.bfloat16
HOP = BF16
LEVELS = 6
MASKS = (1, 2, 6, 8, 16, 48)
PASSED = {0: {(3, 1), (3, 2), (3, 4)}, 1: {(2, 0), (2, 1)}, 2: {(3, 0), (3, 3)}}
EARLY = {
    0: {0: ((3, 0), (1, 0)), 1: ((3, 1), (1, 1)), 2: ((3, 2), (1, 2)), 3: ((3, 3),), 4: ((3, 4), (1, 3), (1, 4))},
    1: {0: ((2, 0),), 1: ((2, 1),), 2: ((2, 2),), 3: ((3, 1),), 4: ((3, 2), (2, 3), (2, 4))},
    2: {4: ((3, 0), (3, 1))},
}
NEXT = 56
PAIRS = tuple((k, j) for k in range(1, LEVELS) for j in range(k, LEVELS))


def dot_nn(a, b):
    return lax.dot_general(a, b, (((1,), (0,)), ((), ())), preferred_element_type=F32)


def dot_nt(a, b):
    return lax.dot_general(a, b, (((1,), (1,)), ((), ())), preferred_element_type=F32)


def halves(value):
    high = value.astype(BF16)
    return high, (value - high.astype(F32)).astype(BF16)


def wide(value):
    high, low = halves(value)
    return jnp.concatenate([high, low, high], axis=1)


def kernel(
    rhs, inv, pan, pat, off, sinv, slink, srhs, x_out, sol_out,
    rhs_v, inv_v, big, sinv_v, slink_v, srhs_v,
    bt, fp, fsnd, frx, cc, cb, prl, psum, prx, pon, meta, metarx, est,
    wf, wi, wg, rt, u, fs, bs, tsnd, trx, ball, solt, soth, sall, acc, xt,
    ld, f_ss, f_rs, p_ss, p_rs, prx_rs, m_ss, m_rs, t_ss, t_rs, b_ss, b_rs, s_ss, s_rs, g_ss, g_rs, o_s,
):
    leaf = lax.axis_index("leaf")
    c = lax.axis_index("col")
    q = lax.rem(leaf, 2)
    base = leaf - q
    c1, c2, c3 = lax.rem(c + 1, 4), lax.rem(c + 2, 4), lax.rem(c + 3, 4)
    rows = 512

    def remote(src, dst, ss, rs, to_leaf, to_col):
        return pltpu.make_async_remote_copy(
            src_ref=src, dst_ref=dst, send_sem=ss, recv_sem=rs,
            device_id=(to_leaf, to_col), device_id_type=MESH,
        )

    sent = []

    def on(cond, fn):
        pl.when(cond)(fn)

    def order(step):
        return jnp.where(c == 0, (2, 1, 3, 0)[step], 3 - step)

    load_rhs = pltpu.make_async_copy(rhs, rhs_v, ld.at[0])
    load_rhs.start()
    load_inv = []
    for step in range(4):
        r = jnp.maximum(order(step), 0)
        load_inv.append(
            pltpu.make_async_copy(inv.at[pl.ds(pl.multiple_of(r * rows, rows), rows)], inv_v.at[r], ld.at[1 + step])
        )
        on(step <= 3 - c, load_inv[step].start)
    peers = [(leaf, c1), (leaf, c2), (leaf, c3)]
    peers += [(base + 1 - q, cc_) for cc_ in (c, c1, c2, c3)]
    peers += [(leaf ^ MASKS[k], c) for k in range(1, LEVELS)]
    z = lax.div(leaf, 8)
    sends_last = (z == 0) | (z == 3) | (z == 4) | (z == 7)
    barrier = pltpu.get_barrier_semaphore()
    for peer in peers:
        pl.semaphore_signal(barrier, inc=1, device_id=peer, device_id_type=MESH)

    def greet_last():
        pl.semaphore_signal(barrier, inc=1, device_id=(leaf ^ NEXT, c), device_id_type=MESH)

    on(sends_last, greet_last)

    for k in range(LEVELS):
        meta[pl.ds(k, 1), :] = jnp.full((1, 256), off[0, k].astype(F32), F32)
        meta[pl.ds(8 + k, 1), :] = jnp.full((1, 256), pat[0, k].astype(F32), F32)

    load_rhs.wait()
    bt[...] = rhs_v[...].T
    other = base + 1 - q
    send_meta = remote(meta, metarx, m_ss, m_rs, other, c)

    def fmsg(sender, number, src, slot, to_col):
        return (c == sender, remote(src, frx.at[slot], f_ss.at[number], f_rs.at[slot], leaf, to_col))

    msgs = {}

    def messages(sender, to_col, items):
        for step, n, slot in items:
            number = sum(1 for key in msgs if key[0] == sender)
            msgs[sender, to_col, step, n] = fmsg(sender, number, fsnd.at[step, n], slot, to_col)

    messages(0, 1, [(0, 0, 0), (0, 1, 1), (1, 0, 2), (1, 1, 3), (1, 2, 4), (1, 3, 5)])
    messages(0, 3, [(0, 2, 0), (0, 3, 1), (2, 2, 4), (2, 3, 5), (2, 0, 2), (2, 1, 3)])
    messages(1, 0, [(0, 0, 0), (0, 1, 1)])
    messages(1, 2, [(0, 2, 0), (0, 3, 1), (1, 2, 4), (1, 3, 5), (1, 0, 2), (1, 1, 3)])
    messages(2, 3, [(0, 0, 6), (0, 1, 7), (0, 2, 8), (0, 3, 9)])
    msgs[3, 2, 9, 0] = fmsg(3, 0, frx.at[0], 6, 2)
    msgs[3, 2, 9, 1] = fmsg(3, 1, frx.at[1], 7, 2)
    later = {(0, 3, 2, 0), (0, 3, 2, 1), (1, 2, 1, 0), (1, 2, 1, 1), (2, 3, 0, 2), (2, 3, 0, 3)}

    def go(step, h):
        for key, (cond, copy) in msgs.items():
            if key[2] == step and key[3] // 2 == h and key not in later:
                on(cond, copy.start)

    for step in range(4):

        def block(step=step):
            load_inv[step].wait()
            r = order(step)
            for h in range(2):
                value = dot_nt(bt[pl.ds(h * 256, 256), :], inv_v[r]).reshape(2, 128, 512)
                fp[step, pl.ds(2 * h, 2)] = value
                if step < 3:
                    fsnd[step, pl.ds(2 * h, 2)] = value.astype(BF16)
                if step > 0:
                    go(step, h)

        on(step <= 3 - c, block)
        if step == 0:
            load_pan = pltpu.make_async_copy(pan, big.at[c, pl.ds(0, 3)], ld.at[5])
            load_pan.start()
            load_sinv = pltpu.make_async_copy(sinv, sinv_v, ld.at[6])
            load_sinv.start()
            load_slink = pltpu.make_async_copy(slink, slink_v, ld.at[7])
            load_slink.start()
            load_srhs = pltpu.make_async_copy(
                srhs.at[:, :, pl.ds(pl.multiple_of(c * 128, 128), 128)], srhs_v, ld.at[8]
            )
            load_srhs.start()
            pl.semaphore_wait(barrier, len(peers) + sends_last.astype(jnp.int32))
            for h in range(2):
                go(0, h)
            send_meta.start()

    load_pan.wait()
    flows = []

    def flow(sender, number, r, p, to_col):
        copy = remote(big.at[r, p], big.at[r, p], g_ss.at[number], g_rs.at[r, p], leaf, to_col)
        flows.append((c == sender, copy))
        return flows[-1]

    def arrive(r, p):
        remote(big.at[r, p], big.at[r, p], g_ss.at[0], g_rs.at[r, p], leaf, c1).wait_recv()

    def start(*items):
        for cond, copy in items:
            on(cond, copy.start)

    def forward(cond, steps):
        def run():
            for r, p, (_, copy) in steps:
                arrive(r, p)
                copy.start()

        on(cond, run)

    start(*(flow(3, p, 3, p, 0) for p in range(3)), flow(3, 3, 3, 0, 2))
    start(*(flow(2, p, 2, p, 1) for p in range(3)), flow(2, 3, 2, 2, 3))
    start(flow(1, 0, 1, 0, 0), flow(1, 1, 1, 1, 0))
    second = flow(3, 4, 3, 1, 2)

    load_sinv.wait()
    load_slink.wait()
    load_srhs.wait()
    highest = lax.Precision.HIGHEST

    def table(k, carry):
        ik = sinv_v[k]
        kk = jnp.minimum(k, LEVELS - 2)
        gk = lax.dot_general(
            slink_v[kk], ik, (((1,), (0,)), ((), ())), precision=highest, preferred_element_type=F32
        )
        hk = lax.dot_general(ik, ik, (((0,), (0,)), ((), ())), precision=highest, preferred_element_type=F32)
        gh, gl = halves(gk)
        hh, hl = halves(hk)
        wf[k, :, pl.ds(0, 256)] = gh
        wf[k, :, pl.ds(256, 256)] = gh
        wf[k, :, pl.ds(512, 256)] = gl
        for ref, (hi, lo) in ((wi, (hh, hl)), (wg, (gh, gl))):
            ref[k, pl.ds(0, 256), :] = hi
            ref[k, pl.ds(256, 256), :] = hi
            ref[k, pl.ds(512, 256), :] = lo
        rt[k] = srhs_v[k].T
        return carry

    lax.fori_loop(0, LEVELS, table, 0)

    send_meta.wait_recv()
    gap = (
        lax.broadcasted_iota(jnp.int32, (128, 256), 1) - lax.broadcasted_iota(jnp.int32, (128, 256), 0)
    ).astype(F32)
    for k in range(LEVELS):
        for part, ref in enumerate((meta, metarx)):
            spot = jnp.broadcast_to(ref[pl.ds(k, 1), :], (128, 256))
            keep = jnp.broadcast_to(ref[pl.ds(8 + k, 1), :], (128, 256))
            hot = jnp.where(gap == spot, keep, 0.0).astype(BF16)
            est[k, pl.ds(part * 256, 128), :] = hot
            est[k, pl.ds(part * 256 + 128, 128), :] = hot

    def product(r, p):
        return dot_nn(big[r, p], inv_v[r])

    def frecv(slot, from_col):
        remote(frx.at[slot], frx.at[slot], f_ss.at[0], f_rs.at[slot], leaf, from_col).wait_recv()

    def got(slot, from_col):
        frecv(slot, from_col)
        return frx[slot].astype(F32)

    def add_and_send(key, slot, from_col):
        _, _, step, n = key
        fsnd[step, n] = (fp[step, n] + got(slot, from_col)).astype(BF16)
        msgs[key][1].start()

    def solved(r, n, value):
        big[r, 3 + n // 2, pl.ds(n % 2 * 128, 128), :] = value.astype(BF16)

    def after0():
        add_and_send((0, 3, 2, 0), 0, 1)
        add_and_send((0, 3, 2, 1), 1, 1)
        for n in range(4):
            solved(0, n, fp[3, n])

    def after1():
        add_and_send((1, 2, 1, 0), 0, 0)
        add_and_send((1, 2, 1, 1), 1, 0)
        for n in range(4):
            solved(1, n, fp[2, n] + got(2 + n, 0))

    def after2():
        add_and_send((2, 3, 0, 2), 0, 1)
        add_and_send((2, 3, 0, 3), 1, 1)
        for n in (2, 3):
            solved(2, n, fp[1, n] + got(2 + n, 1) + got(4 + n, 3))
        for n in (0, 1):
            solved(2, n, fp[1, n] + got(2 + n, 1))

    def after3():
        for n in range(2):
            frecv(n, 0)
            msgs[3, 2, 9, n][1].start()
        second[1].start()
        for n in (2, 3, 0, 1):
            solved(3, n, fp[0, n] + got(6 + n, 2) + got(2 + n, 0))

    for group, fn in enumerate((after0, after1, after2, after3)):
        on(c == group, fn)

    panels = big[c, pl.ds(0, 3)].reshape(768, 512)

    def share(j):
        rows_j = pl.ds(pl.multiple_of(lax.rem(j, 2) * 128, 128), 128)
        value = dot_nt(big[c, 3 + lax.div(j, 2), rows_j, :], panels).reshape(2, 64, 768)
        cc[j] = value
        cb[j] = value.astype(BF16)

    relay_up = remote(cb.at[c2, 0], prl.at[0], p_ss.at[0], p_rs.at[0], leaf, c1)
    relay_down = remote(cb.at[c2, 1], prl.at[1], p_ss.at[1], p_rs.at[1], leaf, c3)
    direct_up = remote(cb.at[c1, 1], prx.at[q, 0], p_ss.at[2], prx_rs.at[q, 0], base + 1, c1)
    direct_down = remote(cb.at[c3, 0], prx.at[q, 1], p_ss.at[3], prx_rs.at[q, 1], base, c3)
    across = remote(cb.at[c, 1 - q], pon, p_ss.at[4], p_rs.at[2], other, c)
    sum_up = remote(psum.at[0], prx.at[q, 0], p_ss.at[5], prx_rs.at[q, 0], base, c1)
    sum_down = remote(psum.at[1], prx.at[q, 1], p_ss.at[6], prx_rs.at[q, 1], base + 1, c3)
    share(c2)
    relay_up.start()
    relay_down.start()
    share(c1)
    direct_up.start()
    share(c3)
    direct_down.start()
    share(c)
    across.start()
    relay_up.wait_recv()
    psum[0] = (cc[c1, 0] + prl[0].astype(F32)).astype(BF16)
    sum_up.start()
    relay_down.wait_recv()
    psum[1] = (cc[c3, 1] + prl[1].astype(F32)).astype(BF16)
    sum_down.start()
    start(flow(3, 5, 3, 3, 0), flow(3, 6, 3, 4, 0), flow(3, 7, 3, 2, 2), flow(3, 8, 3, 3, 2), flow(3, 9, 3, 4, 2))
    start(flow(2, 4, 2, 3, 1), flow(2, 5, 2, 4, 1), flow(2, 6, 2, 3, 3), flow(2, 7, 2, 4, 3))
    start(flow(1, 2, 1, 2, 0), flow(1, 3, 1, 3, 0), flow(1, 4, 1, 4, 0))
    forward(c == 3, [(2, 2, flow(3, 10, 2, 2, 0))])
    forward(c == 2, [(3, 0, flow(2, 8, 3, 0, 1))])
    forward(c == 1, [(2, 0, flow(1, 5, 2, 0, 0)), (2, 1, flow(1, 6, 2, 1, 0))])
    forward(c == 0, [(3, 1, flow(0, 0, 3, 1, 1)), (3, 2, flow(0, 1, 3, 2, 1))])
    across.wait_recv()

    def precv(p, d, from_col):
        remote(prx.at[p, d], prx.at[p, d], p_ss.at[0], prx_rs.at[p, d], base + p, from_col).wait_recv()

    for p in range(2):
        precv(p, 0, c3)
        precv(p, 1, c1)
    mine = cc[c, q] + prx[q, 0].astype(F32) + prx[q, 1].astype(F32)
    theirs = pon[...].astype(F32) + prx[1 - q, 0].astype(F32) + prx[1 - q, 1].astype(F32)
    mh, ml = halves(mine)
    th, tl = halves(theirs)

    def place(k):
        at = slice(k * 128, k * 128 + 128)
        left = jnp.concatenate([mh[:, at], ml[:, at], th[:, at], tl[:, at]], axis=1)
        u[k] = dot_nn(left, est[k])

    mine_rows = pl.ds(pl.multiple_of(q * 64, 64), 64)

    def tree(k, j):
        n = PAIRS.index((k, j))
        return remote(tsnd.at[n], trx.at[n], t_ss.at[n], t_rs.at[n], leaf ^ MASKS[k], c)

    last = len(PAIRS) - 1
    last_near = remote(tsnd.at[last], trx.at[last], t_ss.at[last + 1], t_rs.at[last], leaf ^ NEXT, c)

    def send(k, j):
        tsnd[PAIRS.index((k, j))] = u[j].astype(HOP)
        if k + 1 < LEVELS:
            tree(k, j).start()
        else:
            on(sends_last, last_near.start)
            on(sends_last, tree(k, j).start)

    def receive(k, j):
        tree(k, j).wait_recv()
        u[j] = u[j] + trx[PAIRS.index((k, j))].astype(F32)

    place(0)
    for k in range(LEVELS):
        if k > 0:
            receive(k, k)
        right = wide(rt[k, mine_rows, :] - u[k])
        if k + 1 < LEVELS:
            linked = dot_nt(right, wf[k])
            if k > 0:
                receive(k, k + 1)
            else:
                place(1)
            u[k + 1] = u[k + 1] + linked
            send(k + 1, k + 1)
            for j in range(k + 2, LEVELS):
                if k > 0:
                    receive(k, j)
                else:
                    place(j)
                send(k + 1, j)
        fs[k] = dot_nn(right, wi[k])
        if k < 5:
            acc[k] = product(c, k)
        if k == 3:
            forward(c == 3, [(2, 3, flow(3, 11, 2, 3, 0)), (2, 4, flow(3, 12, 2, 4, 0))])
            forward(c == 2, [(3, 3, flow(2, 9, 3, 3, 1))])
            forward(c == 0, [(3, 4, flow(0, 2, 3, 4, 1))])
        for group, windows in EARLY.items():
            if k in windows:

                def early(group=group, pieces=windows[k]):
                    for r, p in pieces:
                        if (r, p) not in PASSED[group]:
                            arrive(r, p)
                        acc[p] += product(r, p)

                on(c == group, early)
    slot = c * 2 + q
    near, far = jnp.where(q == 0, c3, c1), jnp.where(q == 0, c1, c3)
    swap = remote(ball.at[:, mine_rows, :], ball.at[:, mine_rows, :], b_ss, b_rs, other, c)
    s_copies = []

    def block_of(ref, g):
        return ref.at[:, pl.ds(256 * g, 256)]

    for g in (2, 1, 0):
        for k in (2 * g + 1, 2 * g):
            down = fs[k]
            if k + 1 < LEVELS:
                down = down - dot_nn(wide(bs[k + 1]), wg[k])
            bs[k] = down
            ball[k, mine_rows, :] = down
            low = down.astype(BF16)
            at = slice(k * 128, k * 128 + 128)
            sall[slot, :, at] = dot_nt(low, est[k, pl.ds(0, 128), :]).astype(BF16)
            soth[:, at] = dot_nt(low, est[k, pl.ds(256, 128), :]).astype(BF16)
        mine_g, to_g = block_of(sall.at[slot], g), block_of(sall.at[slot], g)
        for n, (src, to_leaf, to_col) in enumerate(
            ((mine_g, leaf, c1), (mine_g, leaf, c3), (block_of(soth, g), other, c1),
             (block_of(soth, g), other, c3), (block_of(soth, g), other, c))
        ):
            s_copies.append(remote(src, to_g, s_ss.at[n, g], s_rs.at[slot, g], to_leaf, to_col))
            s_copies[-1].start()
    swap.start()

    def srecv(at, g, from_leaf, from_col):
        ref = block_of(sall.at[at], g)
        remote(ref, ref, s_ss.at[0, g], s_rs.at[at, g], from_leaf, from_col).wait_recv()

    relays = []
    for g in (2, 1, 0):
        for p in range(2):
            at = near * 2 + p
            srecv(at, g, base + p, near)
            ref = block_of(sall.at[at], g)
            relays.append(remote(ref, ref, s_ss.at[5 + p, g], s_rs.at[at, g], leaf, far))
            relays[-1].start()

    remote(ball.at[:, mine_rows, :], ball.at[:, mine_rows, :], b_ss, b_rs, other, c).wait_send()
    theirs_rows = pl.ds(pl.multiple_of((1 - q) * 64, 64), 64)
    remote(ball.at[:, theirs_rows, :], ball.at[:, theirs_rows, :], b_ss, b_rs, other, c).wait_recv()
    for k in range(LEVELS):
        solt[k] = ball[k].T
    put_sol = pltpu.make_async_copy(solt, sol_out, o_s.at[0])
    put_sol.start()

    for group in range(3):

        def rest(group=group):
            done = {piece for pieces in EARLY.get(group, {}).values() for piece in pieces}
            for r in range(group + 1, 4):
                for p in range(5):
                    if (r, p) not in done:
                        if (r, p) not in PASSED[group]:
                            arrive(r, p)
                        acc[p] += product(r, p)

        on(c == group, rest)

    weights = acc[pl.ds(0, 3)].reshape(768, 512).astype(BF16)
    puts = []

    def final(y):
        taken = sall[pl.ds(2 * y, 2)].reshape(128, 768)
        rows_y = pl.ds(pl.multiple_of(lax.rem(y, 2) * 128, 128), 128)
        to = pl.ds(pl.multiple_of(y * 128, 128), 128)
        value = acc[3 + lax.div(y, 2), rows_y, :] - dot_nn(taken, weights)
        xt[:, to] = value.T.astype(BF16)
        puts.append(pltpu.make_async_copy(xt.at[:, to], x_out.at[:, to], o_s.at[1 + len(puts)]))
        puts[-1].start()

    for g in range(3):
        srecv(c * 2 + 1 - q, g, other, c)
    final(c)
    final(near)
    for p in range(2):
        for g in range(3):
            srecv(far * 2 + p, g, base + p, far)
    final(far)
    for p in range(2):
        for g in range(3):
            srecv(c2 * 2 + p, g, leaf, near)
    final(c2)

    for copy in (send_meta, relay_up, relay_down, direct_up, direct_down, across, sum_up, sum_down, *s_copies, *relays):
        copy.wait_send()
    for k, j in PAIRS[:-1]:
        tree(k, j).wait_send()
    on(sends_last, tree(*PAIRS[-1]).wait_send)
    on(sends_last, last_near.wait_send)
    for cond, copy in (*msgs.values(), *flows):
        on(cond, copy.wait_send)
    put_sol.wait()
    for put in puts:
        put.wait()


def write_out(x, sol, x_out, sol_out, sems):
    copies = [pltpu.make_async_copy(x, x_out, sems.at[0]), pltpu.make_async_copy(sol, sol_out, sems.at[1])]
    for copy in copies:
        copy.start()
    for copy in copies:
        copy.wait()


def on_device(leaf_rhs, leaf_inverse, panels, pattern, offsets, sep_inverse, sep_link, sep_rhs):
    anywhere = pl.BlockSpec(memory_space=pl.ANY)
    in_hbm = functools.partial(pltpu.with_memory_space_constraint, memory_space=pltpu.HBM)
    hbm = pl.BlockSpec(memory_space=pltpu.HBM)
    scalars = pl.BlockSpec(memory_space=pltpu.SMEM)
    dma = pltpu.SemaphoreType.DMA
    messages = len(PAIRS)
    x, sol = pl.pallas_call(
        kernel,
        out_shape=(jax.ShapeDtypeStruct((512, 512), BF16), jax.ShapeDtypeStruct((6, 256, 128), F32)),
        in_specs=[hbm, hbm, hbm, scalars, scalars, hbm, hbm, hbm],
        out_specs=(anywhere, anywhere),
        scratch_shapes=[
            pltpu.VMEM((512, 512), BF16),
            pltpu.VMEM((4, 512, 512), BF16),
            pltpu.VMEM((4, 5, 256, 512), BF16),
            pltpu.VMEM((6, 256, 256), F32),
            pltpu.VMEM((5, 256, 256), F32),
            pltpu.VMEM((6, 256, 128), F32),
            pltpu.VMEM((512, 512), BF16),
            pltpu.VMEM((4, 4, 128, 512), F32),
            pltpu.VMEM((3, 4, 128, 512), BF16),
            pltpu.VMEM((10, 128, 512), BF16),
            pltpu.VMEM((4, 2, 64, 768), F32),
            pltpu.VMEM((4, 2, 64, 768), BF16),
            pltpu.VMEM((2, 64, 768), BF16),
            pltpu.VMEM((2, 64, 768), BF16),
            pltpu.VMEM((2, 2, 64, 768), BF16),
            pltpu.VMEM((64, 768), BF16),
            pltpu.VMEM((16, 256), F32),
            pltpu.VMEM((16, 256), F32),
            pltpu.VMEM((6, 512, 256), BF16),
            pltpu.VMEM((6, 256, 768), BF16),
            pltpu.VMEM((6, 768, 256), BF16),
            pltpu.VMEM((6, 768, 256), BF16),
            pltpu.VMEM((6, 128, 256), F32),
            pltpu.VMEM((6, 64, 256), F32),
            pltpu.VMEM((6, 64, 256), F32),
            pltpu.VMEM((6, 64, 256), F32),
            pltpu.VMEM((messages, 64, 256), HOP),
            pltpu.VMEM((messages, 64, 256), HOP),
            pltpu.VMEM((6, 128, 256), F32),
            pltpu.VMEM((6, 256, 128), F32),
            pltpu.VMEM((64, 768), BF16),
            pltpu.VMEM((8, 64, 768), BF16),
            pltpu.VMEM((5, 256, 512), F32),
            pltpu.VMEM((512, 512), BF16),
            dma((9,)),
            dma((12,)),
            dma((10,)),
            dma((7,)),
            dma((3,)),
            dma((2, 2)),
            dma,
            dma,
            dma((messages + 1,)),
            dma((messages,)),
            dma,
            dma,
            dma((7, 3)),
            dma((8, 3)),
            dma((13,)),
            dma((4, 5)),
            dma((5,)),
        ],
        compiler_params=pltpu.CompilerParams(
            collective_id=0, has_side_effects=True, vmem_limit_bytes=46 * 1024 * 1024
        ),
    )(
        in_hbm(leaf_rhs[0]),
        in_hbm(leaf_inverse[0]),
        in_hbm(panels[0].reshape(3, 256, 512)),
        in_hbm(pattern),
        in_hbm(offsets),
        in_hbm(sep_inverse[0]),
        in_hbm(sep_link[0]),
        in_hbm(sep_rhs[0]),
    )
    x, sol = pl.pallas_call(
        write_out,
        out_shape=(jax.ShapeDtypeStruct((512, 512), BF16), jax.ShapeDtypeStruct((6, 256, 128), F32)),
        in_specs=[anywhere, anywhere],
        out_specs=(anywhere, anywhere),
        scratch_shapes=[dma((2,))],
        compiler_params=pltpu.CompilerParams(vmem_limit_bytes=1024 * 1024),
    )(x, sol)
    return x[None], sol[None]


def solution(mesh):
    in_specs = (
        P("leaf", "col", None),
        P("leaf", None, "col"),
        P("leaf", None, None, "col"),
        P("leaf", None),
        P("leaf", None),
        P("leaf", None, None, None),
        P("leaf", None, None, None),
        P("leaf", None, None, None),
    )
    out_specs = (P("leaf", "col", None), P("leaf", None, None, "col"))
    return jax.shard_map(on_device, mesh=mesh, in_specs=in_specs, out_specs=out_specs, check_vma=False)
```

```python
import functools

import jax
import jax.numpy as jnp
from jax import lax
from jax.experimental import pallas as pl
from jax.experimental.pallas import tpu as pltpu
from jax.sharding import PartitionSpec as P

MESH = pl.DeviceIdType.MESH
F32 = jnp.float32
BF16 = jnp.bfloat16
HOP = BF16
LEVELS = 6
MASKS = (1, 2, 6, 8, 16, 48)
PASSED = {0: {(3, 1), (3, 2), (3, 4)}, 1: {(2, 0), (2, 1)}, 2: {(3, 0), (3, 3)}}
EARLY = {
    0: {0: ((3, 0), (1, 0)), 1: ((3, 1), (1, 1)), 2: ((3, 2), (1, 2)), 3: ((3, 3),), 4: ((3, 4), (1, 3), (1, 4))},
    1: {0: ((2, 0),), 1: ((2, 1),), 2: ((2, 2),), 3: ((3, 1),), 4: ((3, 2), (2, 3), (2, 4))},
    2: {4: ((3, 0), (3, 1))},
}
NEXT = 56
PAIRS = tuple((k, j) for k in range(1, LEVELS) for j in range(k, LEVELS))


def dot_nn(a, b):
    return lax.dot_general(a, b, (((1,), (0,)), ((), ())), preferred_element_type=F32)


def dot_nt(a, b):
    return lax.dot_general(a, b, (((1,), (1,)), ((), ())), preferred_element_type=F32)


def halves(value):
    high = value.astype(BF16)
    return high, (value - high.astype(F32)).astype(BF16)


def wide(value):
    high, low = halves(value)
    return jnp.concatenate([high, low, high], axis=1)


def kernel(
    rhs, inv, pan, pat, off, sinv, slink, srhs, x_out, sol_out,
    rhs_v, inv_v, big, sinv_v, slink_v, srhs_v,
    bt, fp, fsnd, frx, cc, cb, prl, psum, prx, pon, meta, metarx, est,
    wf, wi, wg, rt, u, fs, bs, tsnd, trx, ball, solt, soth, sall, acc, xt,
    ld, f_ss, f_rs, p_ss, p_rs, prx_rs, m_ss, m_rs, t_ss, t_rs, b_ss, b_rs, s_ss, s_rs, g_ss, g_rs, o_s,
):
    leaf = lax.axis_index("leaf")
    c = lax.axis_index("col")
    q = lax.rem(leaf, 2)
    base = leaf - q
    c1, c2, c3 = lax.rem(c + 1, 4), lax.rem(c + 2, 4), lax.rem(c + 3, 4)
    rows = 512

    def remote(src, dst, ss, rs, to_leaf, to_col):
        return pltpu.make_async_remote_copy(
            src_ref=src, dst_ref=dst, send_sem=ss, recv_sem=rs,
            device_id=(to_leaf, to_col), device_id_type=MESH,
        )

    sent = []

    def on(cond, fn):
        pl.when(cond)(fn)

    def order(step):
        return jnp.where(c == 0, (2, 1, 3, 0)[step], 3 - step)

    load_rhs = pltpu.make_async_copy(rhs, rhs_v, ld.at[0])
    load_rhs.start()
    load_inv = []
    for step in range(4):
        r = jnp.maximum(order(step), 0)
        load_inv.append(
            pltpu.make_async_copy(inv.at[pl.ds(pl.multiple_of(r * rows, rows), rows)], inv_v.at[r], ld.at[1 + step])
        )
        on(step <= 3 - c, load_inv[step].start)
    peers = [(leaf, c1), (leaf, c2), (leaf, c3)]
    peers += [(base + 1 - q, cc_) for cc_ in (c, c1, c2, c3)]
    peers += [(leaf ^ MASKS[k], c) for k in range(1, LEVELS)]
    z = lax.div(leaf, 8)
    sends_last = (z == 0) | (z == 3) | (z == 4) | (z == 7)
    barrier = pltpu.get_barrier_semaphore()
    for peer in peers:
        pl.semaphore_signal(barrier, inc=1, device_id=peer, device_id_type=MESH)

    def greet_last():
        pl.semaphore_signal(barrier, inc=1, device_id=(leaf ^ NEXT, c), device_id_type=MESH)

    on(sends_last, greet_last)

    for k in range(LEVELS):
        meta[pl.ds(k, 1), :] = jnp.full((1, 256), off[0, k].astype(F32), F32)
        meta[pl.ds(8 + k, 1), :] = jnp.full((1, 256), pat[0, k].astype(F32), F32)

    load_rhs.wait()
    bt[...] = rhs_v[...].T
    other = base + 1 - q
    send_meta = remote(meta, metarx, m_ss, m_rs, other, c)

    def fmsg(sender, number, src, slot, to_col):
        return (c == sender, remote(src, frx.at[slot], f_ss.at[number], f_rs.at[slot], leaf, to_col))

    msgs = {}

    def messages(sender, to_col, items):
        for step, n, slot in items:
            number = sum(1 for key in msgs if key[0] == sender)
            msgs[sender, to_col, step, n] = fmsg(sender, number, fsnd.at[step, n], slot, to_col)

    messages(0, 1, [(0, 0, 0), (0, 1, 1), (1, 0, 2), (1, 1, 3), (1, 2, 4), (1, 3, 5)])
    messages(0, 3, [(0, 2, 0), (0, 3, 1), (2, 2, 4), (2, 3, 5), (2, 0, 2), (2, 1, 3)])
    messages(1, 0, [(0, 0, 0), (0, 1, 1)])
    messages(1, 2, [(0, 2, 0), (0, 3, 1), (1, 2, 4), (1, 3, 5), (1, 0, 2), (1, 1, 3)])
    messages(2, 3, [(0, 0, 6), (0, 1, 7), (0, 2, 8), (0, 3, 9)])
    msgs[3, 2, 9, 0] = fmsg(3, 0, frx.at[0], 6, 2)
    msgs[3, 2, 9, 1] = fmsg(3, 1, frx.at[1], 7, 2)
    later = {(0, 3, 2, 0), (0, 3, 2, 1), (1, 2, 1, 0), (1, 2, 1, 1), (2, 3, 0, 2), (2, 3, 0, 3)}

    def go(step, h):
        for key, (cond, copy) in msgs.items():
            if key[2] == step and key[3] // 2 == h and key not in later:
                on(cond, copy.start)

    for step in range(4):

        def block(step=step):
            load_inv[step].wait()
            r = order(step)
            for h in range(2):
                value = dot_nt(bt[pl.ds(h * 256, 256), :], inv_v[r]).reshape(2, 128, 512)
                fp[step, pl.ds(2 * h, 2)] = value
                if step < 3:
                    fsnd[step, pl.ds(2 * h, 2)] = value.astype(BF16)
                if step > 0:
                    go(step, h)

        on(step <= 3 - c, block)
        if step == 0:
            load_pan = pltpu.make_async_copy(pan, big.at[c, pl.ds(0, 3)], ld.at[5])
            load_pan.start()
            load_sinv = pltpu.make_async_copy(sinv, sinv_v, ld.at[6])
            load_sinv.start()
            load_slink = pltpu.make_async_copy(slink, slink_v, ld.at[7])
            load_slink.start()
            load_srhs = pltpu.make_async_copy(
                srhs.at[:, :, pl.ds(pl.multiple_of(c * 128, 128), 128)], srhs_v, ld.at[8]
            )
            load_srhs.start()
            pl.semaphore_wait(barrier, len(peers) + sends_last.astype(jnp.int32))
            for h in range(2):
                go(0, h)
            send_meta.start()

    load_pan.wait()
    flows = []

    def flow(sender, number, r, p, to_col):
        copy = remote(big.at[r, p], big.at[r, p], g_ss.at[number], g_rs.at[r, p], leaf, to_col)
        flows.append((c == sender, copy))
        return flows[-1]

    def arrive(r, p):
        remote(big.at[r, p], big.at[r, p], g_ss.at[0], g_rs.at[r, p], leaf, c1).wait_recv()

    def start(*items):
        for cond, copy in items:
            on(cond, copy.start)

    def forward(cond, steps):
        def run():
            for r, p, (_, copy) in steps:
                arrive(r, p)
                copy.start()

        on(cond, run)

    start(*(flow(3, p, 3, p, 0) for p in range(3)), flow(3, 3, 3, 0, 2))
    start(*(flow(2, p, 2, p, 1) for p in range(3)), flow(2, 3, 2, 2, 3))
    start(flow(1, 0, 1, 0, 0), flow(1, 1, 1, 1, 0), flow(1, 2, 1, 2, 0))
    second = flow(3, 4, 3, 1, 2)

    load_sinv.wait()
    load_slink.wait()
    load_srhs.wait()
    highest = lax.Precision.HIGHEST

    def table(k, carry):
        ik = sinv_v[k]
        kk = jnp.minimum(k, LEVELS - 2)
        gk = lax.dot_general(
            slink_v[kk], ik, (((1,), (0,)), ((), ())), precision=highest, preferred_element_type=F32
        )
        hk = lax.dot_general(ik, ik, (((0,), (0,)), ((), ())), precision=highest, preferred_element_type=F32)
        gh, gl = halves(gk)
        hh, hl = halves(hk)
        wf[k, :, pl.ds(0, 256)] = gh
        wf[k, :, pl.ds(256, 256)] = gh
        wf[k, :, pl.ds(512, 256)] = gl
        for ref, (hi, lo) in ((wi, (hh, hl)), (wg, (gh, gl))):
            ref[k, pl.ds(0, 256), :] = hi
            ref[k, pl.ds(256, 256), :] = hi
            ref[k, pl.ds(512, 256), :] = lo
        rt[k] = srhs_v[k].T
        return carry

    lax.fori_loop(0, LEVELS, table, 0)

    send_meta.wait_recv()
    gap = (
        lax.broadcasted_iota(jnp.int32, (128, 256), 1) - lax.broadcasted_iota(jnp.int32, (128, 256), 0)
    ).astype(F32)
    for k in range(LEVELS):
        for part, ref in enumerate((meta, metarx)):
            spot = jnp.broadcast_to(ref[pl.ds(k, 1), :], (128, 256))
            keep = jnp.broadcast_to(ref[pl.ds(8 + k, 1), :], (128, 256))
            hot = jnp.where(gap == spot, keep, 0.0).astype(BF16)
            est[k, pl.ds(part * 256, 128), :] = hot
            est[k, pl.ds(part * 256 + 128, 128), :] = hot

    def product(r, p):
        return dot_nn(big[r, p], inv_v[r])

    def frecv(slot, from_col):
        remote(frx.at[slot], frx.at[slot], f_ss.at[0], f_rs.at[slot], leaf, from_col).wait_recv()

    def got(slot, from_col):
        frecv(slot, from_col)
        return frx[slot].astype(F32)

    def add_and_send(key, slot, from_col):
        _, _, step, n = key
        fsnd[step, n] = (fp[step, n] + got(slot, from_col)).astype(BF16)
        msgs[key][1].start()

    def solved(r, n, value):
        big[r, 3 + n // 2, pl.ds(n % 2 * 128, 128), :] = value.astype(BF16)

    def after0():
        add_and_send((0, 3, 2, 0), 0, 1)
        add_and_send((0, 3, 2, 1), 1, 1)
        for n in range(4):
            solved(0, n, fp[3, n])

    def after1():
        add_and_send((1, 2, 1, 0), 0, 0)
        add_and_send((1, 2, 1, 1), 1, 0)
        for n in range(4):
            solved(1, n, fp[2, n] + got(2 + n, 0))

    def after2():
        add_and_send((2, 3, 0, 2), 0, 1)
        add_and_send((2, 3, 0, 3), 1, 1)
        for n in (2, 3):
            solved(2, n, fp[1, n] + got(2 + n, 1) + got(4 + n, 3))
        for n in (0, 1):
            solved(2, n, fp[1, n] + got(2 + n, 1))

    def after3():
        for n in range(2):
            frecv(n, 0)
            msgs[3, 2, 9, n][1].start()
        second[1].start()
        for n in (2, 3, 0, 1):
            solved(3, n, fp[0, n] + got(6 + n, 2) + got(2 + n, 0))

    for group, fn in enumerate((after0, after1, after2, after3)):
        on(c == group, fn)

    panels = big[c, pl.ds(0, 3)].reshape(768, 512)

    def share(j):
        rows_j = pl.ds(pl.multiple_of(lax.rem(j, 2) * 128, 128), 128)
        value = dot_nt(big[c, 3 + lax.div(j, 2), rows_j, :], panels).reshape(2, 64, 768)
        cc[j] = value
        cb[j] = value.astype(BF16)

    relay_up = remote(cb.at[c2, 0], prl.at[0], p_ss.at[0], p_rs.at[0], leaf, c1)
    relay_down = remote(cb.at[c2, 1], prl.at[1], p_ss.at[1], p_rs.at[1], leaf, c3)
    direct_up = remote(cb.at[c1, 1], prx.at[q, 0], p_ss.at[2], prx_rs.at[q, 0], base + 1, c1)
    direct_down = remote(cb.at[c3, 0], prx.at[q, 1], p_ss.at[3], prx_rs.at[q, 1], base, c3)
    across = remote(cb.at[c, 1 - q], pon, p_ss.at[4], p_rs.at[2], other, c)
    sum_up = remote(psum.at[0], prx.at[q, 0], p_ss.at[5], prx_rs.at[q, 0], base, c1)
    sum_down = remote(psum.at[1], prx.at[q, 1], p_ss.at[6], prx_rs.at[q, 1], base + 1, c3)
    share(c2)
    relay_up.start()
    relay_down.start()
    share(c1)
    direct_up.start()
    share(c3)
    direct_down.start()
    share(c)
    across.start()
    relay_up.wait_recv()
    psum[0] = (cc[c1, 0] + prl[0].astype(F32)).astype(BF16)
    sum_up.start()
    relay_down.wait_recv()
    psum[1] = (cc[c3, 1] + prl[1].astype(F32)).astype(BF16)
    sum_down.start()
    start(flow(3, 5, 3, 3, 0), flow(3, 6, 3, 4, 0), flow(3, 7, 3, 2, 2), flow(3, 8, 3, 3, 2), flow(3, 9, 3, 4, 2))
    start(flow(2, 4, 2, 3, 1), flow(2, 5, 2, 4, 1), flow(2, 6, 2, 3, 3), flow(2, 7, 2, 4, 3))
    start(flow(1, 3, 1, 3, 0), flow(1, 4, 1, 4, 0))
    forward(c == 3, [(2, 2, flow(3, 10, 2, 2, 0))])
    forward(c == 2, [(3, 0, flow(2, 8, 3, 0, 1))])
    forward(c == 1, [(2, 0, flow(1, 5, 2, 0, 0)), (2, 1, flow(1, 6, 2, 1, 0))])
    forward(c == 0, [(3, 1, flow(0, 0, 3, 1, 1)), (3, 2, flow(0, 1, 3, 2, 1))])
    across.wait_recv()

    def precv(p, d, from_col):
        remote(prx.at[p, d], prx.at[p, d], p_ss.at[0], prx_rs.at[p, d], base + p, from_col).wait_recv()

    for p in range(2):
        precv(p, 0, c3)
        precv(p, 1, c1)
    mine = cc[c, q] + prx[q, 0].astype(F32) + prx[q, 1].astype(F32)
    theirs = pon[...].astype(F32) + prx[1 - q, 0].astype(F32) + prx[1 - q, 1].astype(F32)
    mh, ml = halves(mine)
    th, tl = halves(theirs)

    def place(k):
        at = slice(k * 128, k * 128 + 128)
        left = jnp.concatenate([mh[:, at], ml[:, at], th[:, at], tl[:, at]], axis=1)
        u[k] = dot_nn(left, est[k])

    mine_rows = pl.ds(pl.multiple_of(q * 64, 64), 64)

    def tree(k, j):
        n = PAIRS.index((k, j))
        return remote(tsnd.at[n], trx.at[n], t_ss.at[n], t_rs.at[n], leaf ^ MASKS[k], c)

    last = len(PAIRS) - 1
    last_near = remote(tsnd.at[last], trx.at[last], t_ss.at[last + 1], t_rs.at[last], leaf ^ NEXT, c)

    def send(k, j):
        tsnd[PAIRS.index((k, j))] = u[j].astype(HOP)
        if k + 1 < LEVELS:
            tree(k, j).start()
        else:
            on(sends_last, last_near.start)
            on(sends_last, tree(k, j).start)

    def receive(k, j):
        tree(k, j).wait_recv()
        u[j] = u[j] + trx[PAIRS.index((k, j))].astype(F32)

    place(0)
    for k in range(LEVELS):
        if k > 0:
            receive(k, k)
        right = wide(rt[k, mine_rows, :] - u[k])
        if k + 1 < LEVELS:
            linked = dot_nt(right, wf[k])
            if k > 0:
                receive(k, k + 1)
            else:
                place(1)
            u[k + 1] = u[k + 1] + linked
            send(k + 1, k + 1)
            for j in range(k + 2, LEVELS):
                if k > 0:
                    receive(k, j)
                else:
                    place(j)
                send(k + 1, j)
        fs[k] = dot_nn(right, wi[k])
        if k < 5:
            acc[k] = product(c, k)
        if k == 2:
            forward(c == 3, [(2, 3, flow(3, 11, 2, 3, 0)), (2, 4, flow(3, 12, 2, 4, 0))])
            forward(c == 2, [(3, 3, flow(2, 9, 3, 3, 1))])
            forward(c == 0, [(3, 4, flow(0, 2, 3, 4, 1))])
        for group, windows in EARLY.items():
            if k in windows:

                def early(group=group, pieces=windows[k]):
                    for r, p in pieces:
                        if (r, p) not in PASSED[group]:
                            arrive(r, p)
                        acc[p] += product(r, p)

                on(c == group, early)
    slot = c * 2 + q
    near, far = jnp.where(q == 0, c3, c1), jnp.where(q == 0, c1, c3)
    swap = remote(ball.at[:, mine_rows, :], ball.at[:, mine_rows, :], b_ss, b_rs, other, c)
    s_copies = []

    def block_of(ref, g):
        return ref.at[:, pl.ds(256 * g, 256)]

    for g in (2, 1, 0):
        for k in (2 * g + 1, 2 * g):
            down = fs[k]
            if k + 1 < LEVELS:
                down = down - dot_nn(wide(bs[k + 1]), wg[k])
            bs[k] = down
            ball[k, mine_rows, :] = down
            low = down.astype(BF16)
            at = slice(k * 128, k * 128 + 128)
            sall[slot, :, at] = dot_nt(low, est[k, pl.ds(0, 128), :]).astype(BF16)
            soth[:, at] = dot_nt(low, est[k, pl.ds(256, 128), :]).astype(BF16)
        mine_g, to_g = block_of(sall.at[slot], g), block_of(sall.at[slot], g)
        for n, (src, to_leaf, to_col) in enumerate(
            ((mine_g, leaf, c1), (mine_g, leaf, c3), (block_of(soth, g), other, c1),
             (block_of(soth, g), other, c3), (block_of(soth, g), other, c))
        ):
            s_copies.append(remote(src, to_g, s_ss.at[n, g], s_rs.at[slot, g], to_leaf, to_col))
            s_copies[-1].start()
    swap.start()

    def srecv(at, g, from_leaf, from_col):
        ref = block_of(sall.at[at], g)
        remote(ref, ref, s_ss.at[0, g], s_rs.at[at, g], from_leaf, from_col).wait_recv()

    relays = []
    for g in (2, 1, 0):
        for p in range(2):
            at = near * 2 + p
            srecv(at, g, base + p, near)
            ref = block_of(sall.at[at], g)
            relays.append(remote(ref, ref, s_ss.at[5 + p, g], s_rs.at[at, g], leaf, far))
            relays[-1].start()

    remote(ball.at[:, mine_rows, :], ball.at[:, mine_rows, :], b_ss, b_rs, other, c).wait_send()
    theirs_rows = pl.ds(pl.multiple_of((1 - q) * 64, 64), 64)
    remote(ball.at[:, theirs_rows, :], ball.at[:, theirs_rows, :], b_ss, b_rs, other, c).wait_recv()
    for k in range(LEVELS):
        solt[k] = ball[k].T
    put_sol = pltpu.make_async_copy(solt, sol_out, o_s.at[0])
    put_sol.start()

    for group in range(3):

        def rest(group=group):
            done = {piece for pieces in EARLY.get(group, {}).values() for piece in pieces}
            for r in range(group + 1, 4):
                for p in range(5):
                    if (r, p) not in done:
                        if (r, p) not in PASSED[group]:
                            arrive(r, p)
                        acc[p] += product(r, p)

        on(c == group, rest)

    weights = acc[pl.ds(0, 3)].reshape(768, 512).astype(BF16)
    puts = []

    def final(y):
        taken = sall[pl.ds(2 * y, 2)].reshape(128, 768)
        rows_y = pl.ds(pl.multiple_of(lax.rem(y, 2) * 128, 128), 128)
        to = pl.ds(pl.multiple_of(y * 128, 128), 128)
        value = acc[3 + lax.div(y, 2), rows_y, :] - dot_nn(taken, weights)
        xt[:, to] = value.T.astype(BF16)
        puts.append(pltpu.make_async_copy(xt.at[:, to], x_out.at[:, to], o_s.at[1 + len(puts)]))
        puts[-1].start()

    for g in range(3):
        srecv(c * 2 + 1 - q, g, other, c)
    final(c)
    final(near)
    for p in range(2):
        for g in range(3):
            srecv(far * 2 + p, g, base + p, far)
    final(far)
    for p in range(2):
        for g in range(3):
            srecv(c2 * 2 + p, g, leaf, near)
    final(c2)

    for copy in (send_meta, relay_up, relay_down, direct_up, direct_down, across, sum_up, sum_down, *s_copies, *relays):
        copy.wait_send()
    for k, j in PAIRS[:-1]:
        tree(k, j).wait_send()
    on(sends_last, tree(*PAIRS[-1]).wait_send)
    on(sends_last, last_near.wait_send)
    for cond, copy in (*msgs.values(), *flows):
        on(cond, copy.wait_send)
    put_sol.wait()
    for put in puts:
        put.wait()


def write_out(x, sol, x_out, sol_out, sems):
    copies = [pltpu.make_async_copy(x, x_out, sems.at[0]), pltpu.make_async_copy(sol, sol_out, sems.at[1])]
    for copy in copies:
        copy.start()
    for copy in copies:
        copy.wait()


def on_device(leaf_rhs, leaf_inverse, panels, pattern, offsets, sep_inverse, sep_link, sep_rhs):
    anywhere = pl.BlockSpec(memory_space=pl.ANY)
    in_hbm = functools.partial(pltpu.with_memory_space_constraint, memory_space=pltpu.HBM)
    hbm = pl.BlockSpec(memory_space=pltpu.HBM)
    scalars = pl.BlockSpec(memory_space=pltpu.SMEM)
    dma = pltpu.SemaphoreType.DMA
    messages = len(PAIRS)
    x, sol = pl.pallas_call(
        kernel,
        out_shape=(jax.ShapeDtypeStruct((512, 512), BF16), jax.ShapeDtypeStruct((6, 256, 128), F32)),
        in_specs=[hbm, hbm, hbm, scalars, scalars, hbm, hbm, hbm],
        out_specs=(anywhere, anywhere),
        scratch_shapes=[
            pltpu.VMEM((512, 512), BF16),
            pltpu.VMEM((4, 512, 512), BF16),
            pltpu.VMEM((4, 5, 256, 512), BF16),
            pltpu.VMEM((6, 256, 256), F32),
            pltpu.VMEM((5, 256, 256), F32),
            pltpu.VMEM((6, 256, 128), F32),
            pltpu.VMEM((512, 512), BF16),
            pltpu.VMEM((4, 4, 128, 512), F32),
            pltpu.VMEM((3, 4, 128, 512), BF16),
            pltpu.VMEM((10, 128, 512), BF16),
            pltpu.VMEM((4, 2, 64, 768), F32),
            pltpu.VMEM((4, 2, 64, 768), BF16),
            pltpu.VMEM((2, 64, 768), BF16),
            pltpu.VMEM((2, 64, 768), BF16),
            pltpu.VMEM((2, 2, 64, 768), BF16),
            pltpu.VMEM((64, 768), BF16),
            pltpu.VMEM((16, 256), F32),
            pltpu.VMEM((16, 256), F32),
            pltpu.VMEM((6, 512, 256), BF16),
            pltpu.VMEM((6, 256, 768), BF16),
            pltpu.VMEM((6, 768, 256), BF16),
            pltpu.VMEM((6, 768, 256), BF16),
            pltpu.VMEM((6, 128, 256), F32),
            pltpu.VMEM((6, 64, 256), F32),
            pltpu.VMEM((6, 64, 256), F32),
            pltpu.VMEM((6, 64, 256), F32),
            pltpu.VMEM((messages, 64, 256), HOP),
            pltpu.VMEM((messages, 64, 256), HOP),
            pltpu.VMEM((6, 128, 256), F32),
            pltpu.VMEM((6, 256, 128), F32),
            pltpu.VMEM((64, 768), BF16),
            pltpu.VMEM((8, 64, 768), BF16),
            pltpu.VMEM((5, 256, 512), F32),
            pltpu.VMEM((512, 512), BF16),
            dma((9,)),
            dma((12,)),
            dma((10,)),
            dma((7,)),
            dma((3,)),
            dma((2, 2)),
            dma,
            dma,
            dma((messages + 1,)),
            dma((messages,)),
            dma,
            dma,
            dma((7, 3)),
            dma((8, 3)),
            dma((13,)),
            dma((4, 5)),
            dma((5,)),
        ],
        compiler_params=pltpu.CompilerParams(
            collective_id=0, has_side_effects=True, vmem_limit_bytes=46 * 1024 * 1024
        ),
    )(
        in_hbm(leaf_rhs[0]),
        in_hbm(leaf_inverse[0]),
        in_hbm(panels[0].reshape(3, 256, 512)),
        in_hbm(pattern),
        in_hbm(offsets),
        in_hbm(sep_inverse[0]),
        in_hbm(sep_link[0]),
        in_hbm(sep_rhs[0]),
    )
    x, sol = pl.pallas_call(
        write_out,
        out_shape=(jax.ShapeDtypeStruct((512, 512), BF16), jax.ShapeDtypeStruct((6, 256, 128), F32)),
        in_specs=[anywhere, anywhere],
        out_specs=(anywhere, anywhere),
        scratch_shapes=[dma((2,))],
        compiler_params=pltpu.CompilerParams(vmem_limit_bytes=1024 * 1024),
    )(x, sol)
    return x[None], sol[None]


def solution(mesh):
    in_specs = (
        P("leaf", "col", None),
        P("leaf", None, "col"),
        P("leaf", None, None, "col"),
        P("leaf", None),
        P("leaf", None),
        P("leaf", None, None, None),
        P("leaf", None, None, None),
        P("leaf", None, None, None),
    )
    out_specs = (P("leaf", "col", None), P("leaf", None, None, "col"))
    return jax.shard_map(on_device, mesh=mesh, in_specs=in_specs, out_specs=out_specs, check_vma=False)
```
